128 devices in a mesh: member: 8 (over x, z_hi), space: 16 (over y, z_lo, core).
Axes of the slice: x: 4, y: 4, z: 4 (z_hi: 2, z_lo: 2; z = z_hi * 2 + z_lo), core: 2. Of those that a mesh axis runs over, the one named last changes fastest.
Arguments:
- prior_samples: float32 [256, 128, 4096], P('member', 'space'), may hold values from -6 to 6
- external_drive: float32 [128, 4096], P('space'), may hold values from -6 to 6
- obs_value: float32 [16, 32, 1024], P('space', 'member'), may hold values from -6 to 6
- obs_index: int32 [16, 32, 1024], P('space', 'member'), may hold values from 0 to 1023
- obs_weight: bfloat16 [16, 32, 1024], P('space', 'member'), may hold values from 0.5 to 8
Outputs:
- analysis: float32 [256, 128, 4096], P('member', 'space')
The draws below stay inside these ranges and needn't reach their ends.
Inputs may be any that keep to these rules, and one draw needn't show every extreme that they name: `obs_index`: the cell is numbered row by row within the region: row times 128 plus column.
All inputs are finite; a program needn't handle non-finite values.
Results may differ from the reference program's by a relative error of at most 0.0017.
Values may be sent and summed in bfloat16 or wider, within the bound.
No kernel may reach another device: no remote copies, remote signals or barrier semaphores. Data moves between devices by JAX's collectives and lax.ppermute only.
A program may use at most 128 MiB of HBM per device.

```python
import math
import jax
import jax.numpy as jnp
from jax import lax

SAMPLE_TOTAL = 256
STRIP_HEIGHT = 8
TILE_WIDTH = 128
OBS = 1024
STEPS = 8
ITERS = 6
ROWS = 128
COLS = 4096
COL_REGIONS = 32
N_SPACE = 16


def place_ends(result, rng, low, high):
    dims = result.shape
    spot = [jax.random.randint(jax.random.fold_in(rng, axis), (), 0, dims[axis]) for axis in range(len(dims))]
    result = result.at[tuple(spot)].set(low)
    longest = dims.index(max(dims))
    spot[longest] = (spot[longest] + 1) % dims[longest]
    return result.at[tuple(spot)].set(high)


def levels(stream_key, shape, pieces, smallest, largest):
    level, own = 1.0, jax.random.fold_in(stream_key, 6)
    for position, shards_of in pieces:
        draws = jnp.exp(jax.random.uniform(jax.random.fold_in(own, position), (shards_of,), jnp.float32, smallest / len(pieces), largest / len(pieces)))
        level = level * jnp.repeat(draws, shape[position] // shards_of).reshape([-1 if axis == position else 1 for axis in range(len(shape))])
    return level


def gaussian(own_key, shape, scale, limit, pieces=(), kind=jnp.bfloat16):
    level = levels(own_key, shape, pieces, -0.22, 0.18) if pieces else 1.0
    values = jax.random.normal(own_key, shape, jnp.float32) * scale * level
    return jnp.minimum(jnp.maximum(values, -limit), limit).astype(kind)


def setup_inputs(seed: int = 0) -> dict:
    splits = jax.random.split(jax.random.key(seed), 6)
    prior_samples = gaussian(splits[0], (SAMPLE_TOTAL, ROWS, COLS), 1.0, 6.0, ((0, 8), (1, 16)), jnp.float32)
    external_drive = gaussian(splits[1], (ROWS, COLS), 1.0, 6.0, ((0, 16),), jnp.float32)
    obs_value = gaussian(splits[2], (N_SPACE, COL_REGIONS, OBS), 1.0, 6.0, ((0, 16), (1, 8)), jnp.float32)
    obs_index = place_ends(jax.random.randint(splits[3], (N_SPACE, COL_REGIONS, OBS), 0, STRIP_HEIGHT * TILE_WIDTH), jax.random.fold_in(splits[3], 1), 0, (STRIP_HEIGHT * TILE_WIDTH) - 1).astype(jnp.int32)
    obs_weight = jnp.clip(jnp.exp(math.log(8.0) - 2.7725887 * jax.random.uniform(splits[4], (N_SPACE, COL_REGIONS, OBS), jnp.float32) ** levels(splits[4], (N_SPACE, COL_REGIONS, OBS), ((0, 16), (1, 8)), -0.2, 0.2)), 0.5, 8.0).astype(jnp.bfloat16)
    return {"prior_samples": prior_samples, "external_drive": external_drive, "obs_value": obs_value, "obs_index": obs_index, "obs_weight": obs_weight}


step_size = 0.1
vertical_diffusion = 4.0
lateral_diffusion = 0.5
damping = 0.5

def sample_prediction(sample_grid_vector, external_drive):
    for step_index in range(STEPS):
        padded = jnp.pad(sample_grid_vector, ((1, 1), (0, 0)))
        upper_rows = padded[:-2]
        lower_rows = padded[2:]
        right_cells = jnp.roll(sample_grid_vector, -1, axis=1)
        left_cells = jnp.roll(sample_grid_vector, 1, axis=1)
        laplace = vertical_diffusion * (upper_rows + lower_rows - 2.0 * sample_grid_vector) + lateral_diffusion * (right_cells + left_cells - 2.0 * sample_grid_vector)
        advect = sample_grid_vector * (right_cells - left_cells + (lower_rows - upper_rows)) * 0.5
        sample_grid_vector = sample_grid_vector + step_size * (laplace - advect - damping * sample_grid_vector + external_drive)
    return sample_grid_vector

def taper_above(row_pos, row_span):
    distance = row_span - row_pos
    return jnp.exp(-2.0 * distance * distance / (row_span * row_span))

def taper_below(row_pos, row_span):
    distance = row_pos + 1.0
    return jnp.exp(-2.0 * distance * distance / (row_span * row_span))

def reference(prior_samples, external_drive, obs_value, obs_index, obs_weight):
    highest = lax.Precision.HIGHEST
    predicted_field = lax.map(lambda sample_grid_vector: sample_prediction(sample_grid_vector, external_drive), prior_samples)
    lateral_tiles = COLS // TILE_WIDTH
    points_within_tile = STRIP_HEIGHT * TILE_WIDTH
    number_tiles = N_SPACE * lateral_tiles
    vertical_strips = predicted_field.reshape(SAMPLE_TOTAL, N_SPACE, STRIP_HEIGHT, lateral_tiles, TILE_WIDTH).transpose(1, 3, 0, 2, 4).reshape(number_tiles, SAMPLE_TOTAL, points_within_tile)
    flat_index = obs_index.reshape(number_tiles, OBS)

    def equivalents(region_pair):
        states, cell_index = region_pair
        picked = jnp.take(states, cell_index, axis=1)
        centre = lax.optimization_barrier(jnp.mean(picked, axis=0))
        return ((picked - centre).astype(jnp.bfloat16), centre)
    anomaly_obs, obs_mean = lax.map(equivalents, (vertical_strips, flat_index))
    innovation = lax.optimization_barrier((obs_value.reshape(number_tiles, OBS) - obs_mean).astype(jnp.bfloat16))
    weights = obs_weight.reshape(number_tiles, OBS).astype(jnp.float32)
    row_pos = (flat_index // TILE_WIDTH).astype(jnp.float32)

    def padded_blocks(array):
        shaped = array.reshape((N_SPACE, lateral_tiles) + array.shape[1:])
        return jnp.pad(shaped, ((1, 1),) + ((0, 0),) * (shaped.ndim - 1))
    near_obs = padded_blocks(anomaly_obs)
    near_weight = padded_blocks(weights)
    near_innov = padded_blocks(innovation)
    near_rows = padded_blocks(row_pos)
    row_span = float(STRIP_HEIGHT)
    identity_k = jnp.eye(SAMPLE_TOTAL, dtype=jnp.float32)

    def analyse(region):
        block_row = region // lateral_tiles
        block_col = region % lateral_tiles
        zero_index = block_row * 0

        def pick(array):
            starts = (block_row, block_col) + (zero_index,) * (array.ndim - 2)
            extent = (3, 1) + array.shape[2:]
            return lax.dynamic_slice(array, starts, extent)[:, 0]
        obs_three = pick(near_obs)
        weight_three = pick(near_weight)
        innov_three = pick(near_innov).astype(jnp.float32)
        rows_three = pick(near_rows)
        weight_sets = (weight_three[0] * taper_above(rows_three[0], row_span), weight_three[1], weight_three[2] * taper_below(rows_three[2], row_span))
        curvature = (SAMPLE_TOTAL - 1.0) * identity_k
        right_side = jnp.zeros((SAMPLE_TOTAL,), jnp.float32)
        for block_index in range(3):
            scaled = (obs_three[block_index].astype(jnp.float32) * weight_sets[block_index]).astype(jnp.bfloat16)
            curvature = curvature + lax.dot_general(scaled, obs_three[block_index], (((1,), (1,)), ((), ())), preferred_element_type=jnp.float32)
            right_side = right_side + jnp.dot(obs_three[block_index].astype(jnp.float32), weight_sets[block_index] * innov_three[block_index], precision=highest)
        frobenius = jnp.sqrt(jnp.sum(curvature * curvature))
        iterate = curvature / frobenius
        inverse = identity_k
        for sweep_index in range(ITERS):
            middle = 1.5 * identity_k - 0.5 * jnp.dot(inverse, iterate, precision=highest)
            iterate = jnp.dot(iterate, middle, precision=highest)
            inverse = jnp.dot(middle, inverse, precision=highest)
        spread = inverse * (jnp.sqrt(SAMPLE_TOTAL - 1.0) / jnp.sqrt(frobenius))
        mean_shift = jnp.dot(inverse, jnp.dot(inverse, right_side, precision=highest), precision=highest) / frobenius
        transform = spread + mean_shift[:, None]
        states = lax.dynamic_index_in_dim(vertical_strips, region, 0, keepdims=False)
        centre = lax.optimization_barrier(jnp.mean(states, axis=0, keepdims=True))
        anomalies = states - centre
        return centre + lax.dot_general(transform, anomalies, (((0,), (0,)), ((), ())), precision=highest)
    analysed = lax.map(analyse, jnp.arange(number_tiles, dtype=jnp.int32))
    return analysed.reshape(N_SPACE, lateral_tiles, SAMPLE_TOTAL, STRIP_HEIGHT, TILE_WIDTH).transpose(2, 0, 3, 1, 4).reshape(SAMPLE_TOTAL, ROWS, COLS)
```

```python
import math
from functools import partial

import jax
import jax.numpy as jnp
from jax import lax
from jax.experimental import pallas as pl
from jax.experimental.pallas import tpu as pltpu
from jax.sharding import Mesh, PartitionSpec as P

STEPS = 8
ITERS = 6
ROWS = 8
LANES = 128
PLANE = 4
F32 = jnp.float32
BF16 = jnp.bfloat16


def lane_index(rows):
    return lax.broadcasted_iota(jnp.int32, (rows, LANES), 1)


def halves(x):
    high = x.astype(BF16)
    return high, (x - high.astype(F32)).astype(BF16)


def thirds(x):
    high = x.astype(BF16)
    rest = x - high.astype(F32)
    mid = rest.astype(BF16)
    return high, mid, (rest - mid.astype(F32)).astype(BF16)


def product(a, b):
    ah, al = halves(a)
    bh, bl = halves(b)
    return jnp.dot(
        jnp.concatenate([ah, ah, al], 1),
        jnp.concatenate([bh, bl, bh], 0),
        preferred_element_type=F32,
    )


def against_rows(a, b):
    return lax.dot_general(a, b, (((1,), (1,)), ((), ())), preferred_element_type=F32)


def pack_kernel(tiles, me_ref, prior, drive, value, index, weight, chunk, extra, stage):
    lane = lane_index(16)
    groups = tiles // PLANE

    def place(tile):
        return lax.rem(tile, PLANE) * groups + tile // PLANE

    def rounding(tile, carry):
        cols = pl.ds(pl.multiple_of(tile * LANES, LANES), LANES)
        left = [jnp.zeros((16, LANES), F32)] * 2
        slot = lax.rem(tile, 2)
        stage[slot] = prior[:, cols]
        for row in range(ROWS):
            cells = jnp.concatenate(
                [stage[slot, pl.ds(row, 8, stride=8)], stage[slot, pl.ds(64 + row, 8, stride=8)]], 0
            )
            wanted = cells + left[row % 2]
            kept = wanted.astype(BF16)
            left[row % 2] = wanted - kept.astype(F32)
            chunk[place(tile), row] = kept
        return carry

    lax.fori_loop(0, tiles, rounding, 0)

    def edges(tile, carry):
        before = place(lax.rem(tile + tiles - 1, tiles))
        after = place(lax.rem(tile + 1, tiles))
        total = jnp.zeros((16, LANES), F32)
        for row in range(ROWS):
            both = jnp.where(
                lane >= LANES // 2, chunk[before, row].astype(F32), chunk[after, row].astype(F32)
            )
            moved = pltpu.roll(both, (16 * row + 8) % LANES, 1)
            total = jnp.where(lane // 16 == row, moved, total)
        chunk[place(tile), ROWS] = total.astype(BF16)
        return carry

    lax.fori_loop(0, tiles, edges, 0)

    @pl.when(pl.program_id(0) == 0)
    def _():
        lane8 = lane_index(8)
        weights = weight[0].astype(F32)
        for part in range(PLANE):
            tile = me_ref[0] * PLANE + part

            def forcing(t):
                return drive[:, pl.ds(pl.multiple_of(lax.rem(t + tiles, tiles) * LANES, LANES), LANES)]

            main = forcing(tile)
            low = pltpu.roll(jnp.where(lane8 >= LANES // 2, forcing(tile - 1), main), 8, 1)
            low = jnp.where(lane8 < 32, low, 0.0)
            high = pltpu.roll(jnp.where(lane8 < LANES // 2, forcing(tile + 1), main), 8, 1)
            high = jnp.where((lane8 < 24) | (lane8 >= 120), high, 0.0)
            low = low + pltpu.roll(low, 32, 1)
            low = low + pltpu.roll(low, 64, 1)
            high = high + pltpu.roll(high, 32, 1)
            high = high + pltpu.roll(high, 64, 1)
            extra[part, 0:1, :] = value[0, part : part + 1, :]
            extra[part, 1:2, :] = index[0, part : part + 1, :].astype(F32)
            extra[part, 2:3, :] = weights[part : part + 1, :]
            for slot, field in ((3, main), (4, low), (5, high)):
                for row in range(ROWS):
                    extra[part, slot : slot + 1, row * LANES : (row + 1) * LANES] = field[row : row + 1]
            extra[part, 6:8, :] = jnp.zeros((2, ROWS * LANES), F32)


def pack(me, prior, drive, value, index, weight):
    members, rows, cols = prior.shape
    tiles = cols // LANES
    obs = value.shape[2]
    half = members // 2
    return pl.pallas_call(
        partial(pack_kernel, tiles),
        grid_spec=pltpu.PrefetchScalarGridSpec(
            num_scalar_prefetch=1,
            grid=(2,),
            in_specs=[
                pl.BlockSpec((half * rows, cols), lambda i, s: (i, 0)),
                pl.BlockSpec((rows, cols), lambda i, s: (0, 0)),
                pl.BlockSpec((1, PLANE, obs), lambda i, s: (0, 0, 0)),
                pl.BlockSpec((1, PLANE, obs), lambda i, s: (0, 0, 0)),
                pl.BlockSpec((1, PLANE, obs), lambda i, s: (0, 0, 0)),
            ],
            out_specs=[
                pl.BlockSpec((tiles, ROWS + 1, half, LANES), lambda i, s: (0, 0, i, 0)),
                pl.BlockSpec((PLANE, 8, ROWS * LANES), lambda i, s: (0, 0, 0)),
            ],
            scratch_shapes=[pltpu.VMEM((2, half * rows, LANES), F32)],
        ),
        out_shape=[
            jax.ShapeDtypeStruct((tiles, ROWS + 1, members, LANES), BF16),
            jax.ShapeDtypeStruct((PLANE, 8, ROWS * LANES), F32),
        ],
        name="pack",
    )(me, prior.reshape(members * rows, cols), drive, value, index, weight)


def forecast_kernel(inside, cells, top, bottom, drive, drive_top, drive_bottom, out, state, force):
    depth = (PLANE + 2) * ROWS
    lane = lane_index(8)

    @pl.when(pl.program_id(0) == 0)
    def _():
        for row in range(depth):
            strip, r = divmod(row, ROWS)
            spot = slice(r * LANES, (r + 1) * LANES)
            for slot in range(3):
                pick = slice(3 + slot, 4 + slot)
                if strip == 0:
                    line = drive_top[pick, spot]
                elif strip == PLANE + 1:
                    line = drive_bottom[pick, spot]
                else:
                    line = drive[strip - 1, pick, spot]
                force[slot, row] = jnp.broadcast_to(line * 0.005, (8, LANES))

    for row in range(depth):
        strip, r = divmod(row, ROWS)
        if strip == 0:
            main, edge = top[0, r], top[0, ROWS]
        elif strip == PLANE + 1:
            main, edge = bottom[0, r], bottom[0, ROWS]
        else:
            main, edge = cells[strip - 1, 0, r], cells[strip - 1, 0, ROWS]
        main = main.astype(F32) * 0.05
        edge = edge.astype(F32) * 0.05
        low = jnp.zeros((8, LANES), F32)
        high = jnp.zeros((8, LANES), F32)
        for k in range(4):
            here = main[8 * k : 8 * k + 8]
            state[k, row] = here
            moved = pltpu.roll(here, 32 * k + 8, 1)
            beside = pltpu.roll(edge[8 * k : 8 * k + 8], (32 * k - 16 * r) % LANES, 1)
            at = (lane - 32 * k + LANES) % LANES
            low = jnp.where(at < 8, beside, jnp.where(at < 24, moved, low))
            high = jnp.where(
                (at < 8) | (at >= 120), moved, jnp.where(at < 16, beside, high)
            )
        state[4, row] = low
        state[5, row] = high

    keep_top, keep_bottom = inside[0], inside[1]

    def group(g, carry):
        kind = jnp.maximum(g - 3, 0)
        for step in range(STEPS):
            first, last = step + 1, depth - 2 - step
            above, here = state[g, first - 1], state[g, first]
            for row in range(first, last + 1):
                below = state[g, row + 1]
                east, west = pltpu.roll(here, LANES - 1, 1), pltpu.roll(here, 1, 1)
                turn = (west - east) + (above - below) + 0.05
                fresh = (
                    force[kind, row]
                    + here * turn
                    + 0.05 * (east + west)
                    + 0.4 * (above + below)
                )
                if row < ROWS:
                    fresh = fresh * keep_top
                if row >= depth - ROWS:
                    fresh = fresh * keep_bottom
                state[g, row] = fresh
                above, here = here, below
        return carry

    lax.fori_loop(0, 6, group, 0)

    outer = (lane < 8) | (lane >= LANES - 8)
    for row in range(ROWS, depth - ROWS):
        strip, r = divmod(row - ROWS, ROWS)
        both = jnp.where(lane % 32 < 8, state[5, row], state[4, row])
        for k in range(4):
            side = pltpu.roll(both, (120 - 32 * k) % LANES, 1)
            out[strip, 8 * k : 8 * k + 8, r * LANES : (r + 1) * LANES] = 20.0 * jnp.where(
                outer, side, state[k, row]
            )


def forecast(inside, cells, top, bottom, drive, drive_top, drive_bottom):
    _, groups, lines, members, _ = cells.shape
    whole = lambda shape: pl.BlockSpec(shape, lambda i: (0,) * len(shape))
    return pl.pallas_call(
        forecast_kernel,
        grid=(groups,),
        in_specs=[
            pl.BlockSpec(memory_space=pltpu.SMEM),
            pl.BlockSpec((PLANE, 1, lines, members, LANES), lambda i: (0, i, 0, 0, 0)),
            pl.BlockSpec((1, lines, members, LANES), lambda i: (i, 0, 0, 0)),
            pl.BlockSpec((1, lines, members, LANES), lambda i: (i, 0, 0, 0)),
            whole(drive.shape),
            whole(drive_top.shape),
            whole(drive_bottom.shape),
        ],
        out_specs=pl.BlockSpec((PLANE, members, ROWS * LANES), lambda i: (0, i, 0)),
        out_shape=jax.ShapeDtypeStruct((PLANE, groups * members, ROWS * LANES), F32),
        scratch_shapes=[
            pltpu.VMEM((6, (PLANE + 2) * ROWS, 8, LANES), F32),
            pltpu.VMEM((3, (PLANE + 2) * ROWS, 8, LANES), F32),
        ],
        name="forecast",
    )(inside, cells, top, bottom, drive, drive_top, drive_bottom)


def to_tile(line):
    return jnp.concatenate([line[:, r * LANES : (r + 1) * LANES] for r in range(ROWS)], 0)


def to_line(tile):
    return jnp.concatenate([tile[r : r + 1] for r in range(ROWS)], 1)


def curvature_kernel(states, obs, own, up, down):
    block = pl.program_id(0)
    blocks = pl.num_programs(0)
    members = states.shape[1]
    cells = states[0]
    centre = jnp.sum(cells, axis=0, keepdims=True) * (1.0 / members)
    anomaly = (cells - centre).astype(BF16)
    value, index, weight = obs[0, 0:1], obs[0, 1:2], obs[0, 2:3]
    row_of = jnp.floor(index * (1.0 / LANES))
    col_of = index - row_of * LANES
    count = index.shape[1]
    in_row = lax.broadcasted_iota(jnp.int32, (ROWS, count), 0).astype(F32) == row_of
    in_col = jnp.where(
        lax.broadcasted_iota(jnp.int32, (LANES, count), 0).astype(F32) == col_of, 1.0, 0.0
    ).astype(BF16)
    parts = jnp.concatenate(thirds(to_tile(centre)), 0)
    seen = jnp.dot(parts, in_col, preferred_element_type=F32)
    seen = (seen[:ROWS] + seen[ROWS : 2 * ROWS]) + seen[2 * ROWS :]
    obs_mean = jnp.sum(jnp.where(in_row, seen, 0.0), axis=0, keepdims=True)
    innovation = (value - obs_mean).astype(BF16).astype(F32)
    pull_high, pull_low = halves(weight * innovation)
    spread = jnp.concatenate(
        [
            jnp.where(in_row, weight, 0.0),
            jnp.where(in_row, pull_high.astype(F32), 0.0),
            jnp.where(in_row, pull_low.astype(F32), 0.0),
        ],
        0,
    ).astype(BF16)
    summed = against_rows(spread, in_col)
    weights = summed[:ROWS]
    pulls = summed[ROWS : 2 * ROWS] + summed[2 * ROWS :]
    row_pos = lax.broadcasted_iota(jnp.int32, (ROWS, LANES), 0).astype(F32)
    span = float(ROWS)
    fall_down = jnp.exp(-2.0 * (span - row_pos) * (span - row_pos) / (span * span))
    fall_up = jnp.exp(-2.0 * (row_pos + 1.0) * (row_pos + 1.0) / (span * span))
    wide = anomaly.astype(F32)
    ones = jnp.ones((ROWS, LANES), F32)
    factors = (ones, fall_up, fall_down)
    terms = [
        against_rows((wide * to_line(weights * f)).astype(BF16), anomaly) for f in factors
    ]
    lines = []
    for f in factors:
        lines.extend(thirds(to_line(pulls * f)))
    lines.append(jnp.zeros((7, count), BF16))
    vectors = against_rows(jnp.concatenate(lines, 0), anomaly)
    sides = [
        (vectors[3 * i : 3 * i + 1] + vectors[3 * i + 1 : 3 * i + 2]) + vectors[3 * i + 2 : 3 * i + 3]
        for i in range(3)
    ]
    pad = jnp.zeros((7, members), F32)

    @pl.when(block == 0)
    def _():
        own[...] = jnp.zeros_like(own)
        up[:members] = terms[1]
        up[members:] = jnp.concatenate([sides[1], pad], 0)

    own[block, :members] += terms[0]
    own[block, members:] += jnp.concatenate([sides[0], pad], 0)

    @pl.when(block > 0)
    def _():
        own[block - 1, :members] += terms[1]
        own[block - 1, members:] += jnp.concatenate([sides[1], pad], 0)

    @pl.when(block < blocks - 1)
    def _():
        own[block + 1, :members] += terms[2]
        own[block + 1, members:] += jnp.concatenate([sides[2], pad], 0)

    @pl.when(block == blocks - 1)
    def _():
        down[:members] = terms[2]
        down[members:] = jnp.concatenate([sides[2], pad], 0)


def curvatures(states, obs):
    blocks, members, width = states.shape
    whole = lambda shape: pl.BlockSpec(shape, lambda i: (0,) * len(shape))
    return pl.pallas_call(
        curvature_kernel,
        grid=(blocks,),
        in_specs=[
            pl.BlockSpec((1, members, width), lambda i: (i, 0, 0)),
            pl.BlockSpec((1, 8, width), lambda i: (i, 0, 0)),
        ],
        out_specs=[
            whole((blocks, members + 8, members)),
            whole((members + 8, members)),
            whole((members + 8, members)),
        ],
        out_shape=[
            jax.ShapeDtypeStruct((blocks, members + 8, members), F32),
            jax.ShapeDtypeStruct((members + 8, members), F32),
            jax.ShapeDtypeStruct((members + 8, members), F32),
        ],
        name="curvature",
    )(states, obs)


def transform_kernel(own, from_above, from_below, out, iterate, inverse):
    blocks, size, _ = iterate.shape
    row = lax.broadcasted_iota(jnp.int32, (size, size), 0)
    col = lax.broadcasted_iota(jnp.int32, (size, size), 1)
    diagonal = row == col

    def middle_of(x):
        return jnp.where(diagonal, 1.5 - 0.5 * x, -0.5 * x)

    norms, sides = [], []
    for b in range(blocks):
        matrix, side = own[b, :size], own[b, size:]
        if b == 0:
            matrix, side = matrix + from_above[:size], side + from_above[size:]
        if b == blocks - 1:
            matrix, side = matrix + from_below[:size], side + from_below[size:]
        matrix = matrix + jnp.where(diagonal, size - 1.0, 0.0)
        squares = jnp.sum(jnp.sum(matrix * matrix, axis=0, keepdims=True), axis=1, keepdims=True)
        norm = jnp.sqrt(squares)
        start = matrix / norm
        middle = middle_of(start)
        inverse[b] = middle
        iterate[b] = product(start, middle)
        norms.append(norm)
        sides.append(side)

    def sweep(i, carry):
        middles = [middle_of(product(inverse[b], iterate[b])) for b in range(blocks)]
        for b in range(blocks):
            both = product(jnp.concatenate([iterate[b], inverse[b]], 0), middles[b])
            iterate[b] = both[:size]
            inverse[b] = both[size:]
        return carry

    lax.fori_loop(0, ITERS - 2, sweep, 0)
    middles = [middle_of(product(inverse[b], iterate[b])) for b in range(blocks)]
    finals = [product(inverse[b], middles[b]) for b in range(blocks)]
    for b in range(blocks):
        flipped = finals[b].T
        inner = product(sides[b], flipped)
        shift = product(inner, flipped) / norms[b]
        out[b, :size] = flipped * (math.sqrt(size - 1.0) / jnp.sqrt(norms[b]))
        out[b, size:] = shift


def transforms(own, from_above, from_below):
    blocks, _, size = own.shape
    return pl.pallas_call(
        transform_kernel,
        out_shape=jax.ShapeDtypeStruct(own.shape, F32),
        scratch_shapes=[
            pltpu.VMEM((blocks, size, size), F32),
            pltpu.VMEM((blocks, size, size), F32),
        ],
        name="transform",
    )(own, from_above, from_below)


def apply_kernel(share, states, weights, out):
    members = states.shape[1]
    cells = states[0]
    centre = jnp.sum(cells, axis=0, keepdims=True) * (1.0 / members)
    moved = product(weights[0], cells - centre)
    common_high, common_low = halves(centre + moved[members : members + 1])
    common = jnp.concatenate(
        [to_tile(common_high.astype(F32)), to_tile(common_low.astype(F32))], 0
    ).astype(BF16)
    for part in range(members // share):
        for r in range(ROWS):
            out[0, part, r * share : (r + 1) * share] = moved[
                part * share : (part + 1) * share, r * LANES : (r + 1) * LANES
            ].astype(BF16)
        out[0, part, ROWS * share :] = common


def apply_transform(share, states, weights):
    blocks, members, width = states.shape
    lines = ROWS * share + 16
    return pl.pallas_call(
        partial(apply_kernel, share),
        grid=(blocks,),
        in_specs=[
            pl.BlockSpec((1, members, width), lambda i: (i, 0, 0)),
            pl.BlockSpec((1, members + 8, members), lambda i: (i, 0, 0)),
        ],
        out_specs=pl.BlockSpec((1, members // share, lines, LANES), lambda i: (i, 0, 0, 0)),
        out_shape=jax.ShapeDtypeStruct((blocks, members // share, lines, LANES), BF16),
        name="apply",
    )(states, weights)


def unpack_kernel(share, chunk, out, stage):
    for part in range(PLANE):
        cols = slice(part * LANES, (part + 1) * LANES)
        common = chunk[part, 0, ROWS * share :].astype(F32)
        common = common[:ROWS] + common[ROWS:]
        for r in range(ROWS):
            field = chunk[part, 0, r * share : (r + 1) * share].astype(F32) + common[r : r + 1]
            for k in range(share // 8):
                stage[part, pl.ds(64 * k + r, 8, stride=8)] = field[8 * k : 8 * k + 8]
        out[:, cols] = stage[part]


def unpack(share, chunk):
    _, groups, lines, _ = chunk.shape
    return pl.pallas_call(
        partial(unpack_kernel, share),
        grid=(groups,),
        in_specs=[pl.BlockSpec((PLANE, 1, lines, LANES), lambda i: (0, i, 0, 0))],
        out_specs=pl.BlockSpec((share * ROWS, PLANE * LANES), lambda i: (0, i)),
        out_shape=jax.ShapeDtypeStruct((share * ROWS, groups * PLANE * LANES), F32),
        scratch_shapes=[pltpu.VMEM((PLANE, share * ROWS, LANES), F32)],
        name="unpack",
    )(chunk)


def local(prior, drive, value, index, weight):
    members, rows, cols = prior.shape
    groups = lax.axis_size("member")
    planes = lax.axis_size("y")
    plane = lax.axis_index("y")
    upward = [(i + 1, i) for i in range(planes - 1)]
    downward = [(i, i + 1) for i in range(planes - 1)]
    me = lax.axis_index("member").reshape(1).astype(jnp.int32)
    chunk, extra = pack(me, prior, drive, value, index, weight)
    extra = lax.all_to_all(extra, "zc", 0, 0, tiled=True)
    chunk = lax.all_to_all(chunk, ("zc", "member"), 0, 0, tiled=True)
    cells = chunk.reshape(PLANE, groups, ROWS + 1, members, LANES)
    bottom = lax.ppermute(cells[0], "y", upward)
    top = lax.ppermute(cells[PLANE - 1], "y", downward)
    drive_bottom = lax.ppermute(extra[0], "y", upward)
    drive_top = lax.ppermute(extra[PLANE - 1], "y", downward)
    inside = jnp.stack([plane > 0, plane < planes - 1]).astype(F32)
    states = forecast(inside, cells, top, bottom, extra, drive_top, drive_bottom)
    own, up, down = curvatures(states, extra)
    from_below = lax.ppermute(up, "y", upward)
    from_above = lax.ppermute(down, "y", downward)
    weights = transforms(own, from_above, from_below)
    analysed = apply_transform(members, states, weights)
    lines = ROWS * members + 16
    back = lax.all_to_all(
        analysed.reshape(PLANE * groups, lines, LANES), ("zc", "member"), 0, 0, tiled=True
    )
    return unpack(members, back.reshape(PLANE, groups, lines, LANES)).reshape(members, rows, cols)


def solution(mesh):
    groups, spaces = mesh.devices.shape
    fine = Mesh(mesh.devices.reshape(groups, spaces // PLANE, PLANE), ("member", "y", "zc"))
    rows = ("y", "zc")
    return jax.shard_map(
        local,
        mesh=fine,
        in_specs=(
            P("member", rows, None),
            P(rows, None),
            P(rows, "member", None),
            P(rows, "member", None),
            P(rows, "member", None),
        ),
        out_specs=P("member", rows, None),
        check_vma=False,
    )
```

```python
import math
from functools import partial

import jax
import jax.numpy as jnp
from jax import lax
from jax.experimental import pallas as pl
from jax.experimental.pallas import tpu as pltpu
from jax.sharding import Mesh, PartitionSpec as P

STEPS = 8
ITERS = 6
ROWS = 8
LANES = 128
PLANE = 4
F32 = jnp.float32
BF16 = jnp.bfloat16


def lane_index(rows):
    return lax.broadcasted_iota(jnp.int32, (rows, LANES), 1)


def halves(x):
    high = x.astype(BF16)
    return high, (x - high.astype(F32)).astype(BF16)


def thirds(x):
    high = x.astype(BF16)
    rest = x - high.astype(F32)
    mid = rest.astype(BF16)
    return high, mid, (rest - mid.astype(F32)).astype(BF16)


def product(a, b):
    ah, al = halves(a)
    bh, bl = halves(b)
    return jnp.dot(
        jnp.concatenate([ah, ah, al], 1),
        jnp.concatenate([bh, bl, bh], 0),
        preferred_element_type=F32,
    )


def against_rows(a, b):
    return lax.dot_general(a, b, (((1,), (1,)), ((), ())), preferred_element_type=F32)


def pack_kernel(tiles, prior, chunk, stage):
    lane = lane_index(16)
    groups = tiles // PLANE

    def place(tile):
        return lax.rem(tile, PLANE) * groups + tile // PLANE

    def rounding(tile, carry):
        cols = pl.ds(pl.multiple_of(tile * LANES, LANES), LANES)
        left = [jnp.zeros((16, LANES), F32)] * 2
        slot = lax.rem(tile, 2)
        stage[slot] = prior[:, cols]
        for row in range(ROWS):
            cells = jnp.concatenate(
                [stage[slot, pl.ds(row, 8, stride=8)], stage[slot, pl.ds(64 + row, 8, stride=8)]], 0
            )
            wanted = cells + left[row % 2]
            kept = wanted.astype(BF16)
            left[row % 2] = wanted - kept.astype(F32)
            chunk[place(tile), row] = kept
        return carry

    lax.fori_loop(0, tiles, rounding, 0)

    def edges(tile, carry):
        before = place(lax.rem(tile + tiles - 1, tiles))
        after = place(lax.rem(tile + 1, tiles))
        total = jnp.zeros((16, LANES), F32)
        for row in range(ROWS):
            both = jnp.where(
                lane >= LANES // 2, chunk[before, row].astype(F32), chunk[after, row].astype(F32)
            )
            moved = pltpu.roll(both, (16 * row + 8) % LANES, 1)
            total = jnp.where(lane // 16 == row, moved, total)
        chunk[place(tile), ROWS] = total.astype(BF16)
        return carry

    lax.fori_loop(0, tiles, edges, 0)


def extra_kernel(tiles, me_ref, drive, value, index, weight, extra):
    lane8 = lane_index(8)
    weights = weight[0].astype(F32)
    for part in range(PLANE):
        tile = me_ref[0] * PLANE + part

        def forcing(t):
            return drive[:, pl.ds(pl.multiple_of(lax.rem(t + tiles, tiles) * LANES, LANES), LANES)]

        main = forcing(tile)
        low = pltpu.roll(jnp.where(lane8 >= LANES // 2, forcing(tile - 1), main), 8, 1)
        low = jnp.where(lane8 < 32, low, 0.0)
        high = pltpu.roll(jnp.where(lane8 < LANES // 2, forcing(tile + 1), main), 8, 1)
        high = jnp.where((lane8 < 24) | (lane8 >= 120), high, 0.0)
        low = low + pltpu.roll(low, 32, 1)
        low = low + pltpu.roll(low, 64, 1)
        high = high + pltpu.roll(high, 32, 1)
        high = high + pltpu.roll(high, 64, 1)
        extra[part, 0:1, :] = value[0, part : part + 1, :]
        extra[part, 1:2, :] = index[0, part : part + 1, :].astype(F32)
        extra[part, 2:3, :] = weights[part : part + 1, :]
        for slot, field in ((3, main), (4, low), (5, high)):
            for row in range(ROWS):
                extra[part, slot : slot + 1, row * LANES : (row + 1) * LANES] = field[row : row + 1]
        extra[part, 6:8, :] = jnp.zeros((2, ROWS * LANES), F32)


def pack_extra(me, cols, drive, value, index, weight):
    return pl.pallas_call(
        partial(extra_kernel, cols // LANES),
        in_specs=[pl.BlockSpec(memory_space=pltpu.SMEM)]
        + [pl.BlockSpec(memory_space=pltpu.VMEM)] * 4,
        out_shape=jax.ShapeDtypeStruct((PLANE, 8, ROWS * LANES), F32),
        name="pack_extra",
    )(me, drive, value, index, weight)


def pack(prior, half):
    members, rows, cols = prior.shape
    tiles = cols // LANES
    part = members // 2
    return pl.pallas_call(
        partial(pack_kernel, tiles),
        grid=(1,),
        in_specs=[pl.BlockSpec((part * rows, cols), lambda i: (half, 0))],
        out_specs=pl.BlockSpec((tiles, ROWS + 1, part, LANES), lambda i: (0, 0, 0, 0)),
        out_shape=jax.ShapeDtypeStruct((tiles, ROWS + 1, part, LANES), BF16),
        scratch_shapes=[pltpu.VMEM((2, part * rows, LANES), F32)],
        name="pack",
    )(prior.reshape(members * rows, cols))


def forecast_kernel(inside, cells, top, bottom, drive, drive_top, drive_bottom, out, state, force):
    depth = (PLANE + 2) * ROWS
    lane = lane_index(8)

    @pl.when(pl.program_id(0) == 0)
    def _():
        for row in range(depth):
            strip, r = divmod(row, ROWS)
            spot = slice(r * LANES, (r + 1) * LANES)
            for slot in range(3):
                pick = slice(3 + slot, 4 + slot)
                if strip == 0:
                    line = drive_top[pick, spot]
                elif strip == PLANE + 1:
                    line = drive_bottom[pick, spot]
                else:
                    line = drive[strip - 1, pick, spot]
                force[slot, row] = jnp.broadcast_to(line * 0.005, (8, LANES))

    for row in range(depth):
        strip, r = divmod(row, ROWS)
        if strip == 0:
            source = top
        elif strip == PLANE + 1:
            source = bottom
        else:
            source = cells.at[strip - 1]
        main = jnp.concatenate([source[0, r], source[1, r]], 0).astype(F32) * 0.05
        edge = jnp.concatenate([source[0, ROWS], source[1, ROWS]], 0).astype(F32) * 0.05
        low = jnp.zeros((8, LANES), F32)
        high = jnp.zeros((8, LANES), F32)
        for k in range(4):
            here = main[8 * k : 8 * k + 8]
            state[k, row] = here
            moved = pltpu.roll(here, 32 * k + 8, 1)
            beside = pltpu.roll(edge[8 * k : 8 * k + 8], (32 * k - 16 * r) % LANES, 1)
            at = (lane - 32 * k + LANES) % LANES
            low = jnp.where(at < 8, beside, jnp.where(at < 24, moved, low))
            high = jnp.where(
                (at < 8) | (at >= 120), moved, jnp.where(at < 16, beside, high)
            )
        state[4, row] = low
        state[5, row] = high

    keep_top, keep_bottom = inside[0], inside[1]

    def group(g, carry):
        kind = jnp.maximum(g - 3, 0)
        for step in range(STEPS):
            first, last = step + 1, depth - 2 - step
            above, here = state[g, first - 1], state[g, first]
            for row in range(first, last + 1):
                below = state[g, row + 1]
                east, west = pltpu.roll(here, LANES - 1, 1), pltpu.roll(here, 1, 1)
                turn = (west - east) + (above - below) + 0.05
                fresh = (
                    force[kind, row]
                    + here * turn
                    + 0.05 * (east + west)
                    + 0.4 * (above + below)
                )
                if row < ROWS:
                    fresh = fresh * keep_top
                if row >= depth - ROWS:
                    fresh = fresh * keep_bottom
                state[g, row] = fresh
                above, here = here, below
        return carry

    lax.fori_loop(0, 6, group, 0)

    outer = (lane < 8) | (lane >= LANES - 8)
    for row in range(ROWS, depth - ROWS):
        strip, r = divmod(row - ROWS, ROWS)
        both = jnp.where(lane % 32 < 8, state[5, row], state[4, row])
        for k in range(4):
            side = pltpu.roll(both, (120 - 32 * k) % LANES, 1)
            out[strip, 8 * k : 8 * k + 8, r * LANES : (r + 1) * LANES] = 20.0 * jnp.where(
                outer, side, state[k, row]
            )


def forecast(inside, cells, top, bottom, drive, drive_top, drive_bottom, begin, end):
    _, _, lines, members, _ = cells.shape
    at = begin // 2
    whole = lambda shape: pl.BlockSpec(shape, lambda i: (0,) * len(shape))
    return pl.pallas_call(
        forecast_kernel,
        grid=((end - begin) // 2,),
        in_specs=[
            pl.BlockSpec(memory_space=pltpu.SMEM),
            pl.BlockSpec((PLANE, 2, lines, members, LANES), lambda i: (0, i + at, 0, 0, 0)),
            pl.BlockSpec((2, lines, members, LANES), lambda i: (i + at, 0, 0, 0)),
            pl.BlockSpec((2, lines, members, LANES), lambda i: (i + at, 0, 0, 0)),
            whole(drive.shape),
            whole(drive_top.shape),
            whole(drive_bottom.shape),
        ],
        out_specs=pl.BlockSpec((PLANE, 2 * members, ROWS * LANES), lambda i: (0, i, 0)),
        out_shape=jax.ShapeDtypeStruct((PLANE, (end - begin) * members, ROWS * LANES), F32),
        scratch_shapes=[
            pltpu.VMEM((6, (PLANE + 2) * ROWS, 8, LANES), F32),
            pltpu.VMEM((3, (PLANE + 2) * ROWS, 8, LANES), F32),
        ],
        name="forecast",
    )(inside, cells, top, bottom, drive, drive_top, drive_bottom)


def to_tile(line):
    return jnp.concatenate([line[:, r * LANES : (r + 1) * LANES] for r in range(ROWS)], 0)


def to_line(tile):
    return jnp.concatenate([tile[r : r + 1] for r in range(ROWS)], 1)


def curvature_kernel(pieces, *refs):
    states, (obs, own, up, down) = refs[:pieces], refs[pieces:]
    block = pl.program_id(0)
    blocks = pl.num_programs(0)
    cells = jnp.concatenate([piece[0] for piece in states], 0)
    members = cells.shape[0]
    centre = jnp.sum(cells, axis=0, keepdims=True) * (1.0 / members)
    anomaly = (cells - centre).astype(BF16)
    value, index, weight = obs[0, 0:1], obs[0, 1:2], obs[0, 2:3]
    row_of = jnp.floor(index * (1.0 / LANES))
    col_of = index - row_of * LANES
    count = index.shape[1]
    in_row = lax.broadcasted_iota(jnp.int32, (ROWS, count), 0).astype(F32) == row_of
    in_col = jnp.where(
        lax.broadcasted_iota(jnp.int32, (LANES, count), 0).astype(F32) == col_of, 1.0, 0.0
    ).astype(BF16)
    parts = jnp.concatenate(thirds(to_tile(centre)), 0)
    seen = jnp.dot(parts, in_col, preferred_element_type=F32)
    seen = (seen[:ROWS] + seen[ROWS : 2 * ROWS]) + seen[2 * ROWS :]
    obs_mean = jnp.sum(jnp.where(in_row, seen, 0.0), axis=0, keepdims=True)
    innovation = (value - obs_mean).astype(BF16).astype(F32)
    pull_high, pull_low = halves(weight * innovation)
    spread = jnp.concatenate(
        [
            jnp.where(in_row, weight, 0.0),
            jnp.where(in_row, pull_high.astype(F32), 0.0),
            jnp.where(in_row, pull_low.astype(F32), 0.0),
        ],
        0,
    ).astype(BF16)
    summed = against_rows(spread, in_col)
    weights = summed[:ROWS]
    pulls = summed[ROWS : 2 * ROWS] + summed[2 * ROWS :]
    row_pos = lax.broadcasted_iota(jnp.int32, (ROWS, LANES), 0).astype(F32)
    span = float(ROWS)
    fall_down = jnp.exp(-2.0 * (span - row_pos) * (span - row_pos) / (span * span))
    fall_up = jnp.exp(-2.0 * (row_pos + 1.0) * (row_pos + 1.0) / (span * span))
    wide = anomaly.astype(F32)
    ones = jnp.ones((ROWS, LANES), F32)
    factors = (ones, fall_up, fall_down)
    terms = [
        against_rows((wide * to_line(weights * f)).astype(BF16), anomaly) for f in factors
    ]
    lines = []
    for f in factors:
        lines.extend(thirds(to_line(pulls * f)))
    lines.append(jnp.zeros((7, count), BF16))
    vectors = against_rows(jnp.concatenate(lines, 0), anomaly)
    sides = [
        (vectors[3 * i : 3 * i + 1] + vectors[3 * i + 1 : 3 * i + 2]) + vectors[3 * i + 2 : 3 * i + 3]
        for i in range(3)
    ]
    pad = jnp.zeros((7, members), F32)

    @pl.when(block == 0)
    def _():
        own[...] = jnp.zeros_like(own)
        up[:members] = terms[1]
        up[members:] = jnp.concatenate([sides[1], pad], 0)

    own[block, :members] += terms[0]
    own[block, members:] += jnp.concatenate([sides[0], pad], 0)

    @pl.when(block > 0)
    def _():
        own[block - 1, :members] += terms[1]
        own[block - 1, members:] += jnp.concatenate([sides[1], pad], 0)

    @pl.when(block < blocks - 1)
    def _():
        own[block + 1, :members] += terms[2]
        own[block + 1, members:] += jnp.concatenate([sides[2], pad], 0)

    @pl.when(block == blocks - 1)
    def _():
        down[:members] = terms[2]
        down[members:] = jnp.concatenate([sides[2], pad], 0)


def of_block(states):
    return [pl.BlockSpec((1, *piece.shape[1:]), lambda i: (i, 0, 0)) for piece in states]


def curvatures(states, obs):
    blocks, _, width = states[0].shape
    members = sum(piece.shape[1] for piece in states)
    whole = lambda shape: pl.BlockSpec(shape, lambda i: (0,) * len(shape))
    return pl.pallas_call(
        partial(curvature_kernel, len(states)),
        grid=(blocks,),
        in_specs=[*of_block(states), pl.BlockSpec((1, 8, width), lambda i: (i, 0, 0))],
        out_specs=[
            whole((blocks, members + 8, members)),
            whole((members + 8, members)),
            whole((members + 8, members)),
        ],
        out_shape=[
            jax.ShapeDtypeStruct((blocks, members + 8, members), F32),
            jax.ShapeDtypeStruct((members + 8, members), F32),
            jax.ShapeDtypeStruct((members + 8, members), F32),
        ],
        name="curvature",
    )(*states, obs)


def transform_kernel(edges, *refs):
    own, *rest = refs
    *halo, out, iterate, inverse = rest
    blocks, size, _ = iterate.shape
    row = lax.broadcasted_iota(jnp.int32, (size, size), 0)
    col = lax.broadcasted_iota(jnp.int32, (size, size), 1)
    diagonal = row == col

    def middle_of(x):
        return jnp.where(diagonal, 1.5 - 0.5 * x, -0.5 * x)

    norms, sides = [], []
    for b in range(blocks):
        place = b * (own.shape[0] - 1) if edges else b + 1
        matrix, side = own[place, :size], own[place, size:]
        if edges:
            matrix, side = matrix + halo[b][:size], side + halo[b][size:]
        matrix = matrix + jnp.where(diagonal, size - 1.0, 0.0)
        squares = jnp.sum(jnp.sum(matrix * matrix, axis=0, keepdims=True), axis=1, keepdims=True)
        norm = jnp.sqrt(squares)
        start = matrix / norm
        middle = middle_of(start)
        inverse[b] = middle
        iterate[b] = product(start, middle)
        norms.append(norm)
        sides.append(side)

    def sweep(i, carry):
        middles = [middle_of(product(inverse[b], iterate[b])) for b in range(blocks)]
        for b in range(blocks):
            both = product(jnp.concatenate([iterate[b], inverse[b]], 0), middles[b])
            iterate[b] = both[:size]
            inverse[b] = both[size:]
        return carry

    lax.fori_loop(0, ITERS - 2, sweep, 0)
    middles = [middle_of(product(inverse[b], iterate[b])) for b in range(blocks)]
    finals = [product(inverse[b], middles[b]) for b in range(blocks)]
    for b in range(blocks):
        flipped = finals[b].T
        inner = product(sides[b], flipped)
        shift = product(inner, flipped) / norms[b]
        out[b, :size] = flipped * (math.sqrt(size - 1.0) / jnp.sqrt(norms[b]))
        out[b, size:] = shift


def transforms(own, *halo):
    total, lines, size = own.shape
    blocks = len(halo) or total - 2
    return pl.pallas_call(
        partial(transform_kernel, bool(halo)),
        out_shape=jax.ShapeDtypeStruct((blocks, lines, size), F32),
        scratch_shapes=[
            pltpu.VMEM((blocks, size, size), F32),
            pltpu.VMEM((blocks, size, size), F32),
        ],
        name="transform",
    )(own, *halo)


def apply_kernel(share, begin, pieces, *refs):
    states, (inner, outer, out) = refs[:pieces], refs[pieces:]
    block = pl.program_id(0)
    within = (block > 0) & (block < pl.num_programs(0) - 1)
    cells = jnp.concatenate([piece[0] for piece in states], 0)
    members, width = cells.shape
    rows = width // LANES
    half = share // 2
    weights = jnp.where(within, inner[0], outer[0])
    centre = jnp.sum(cells, axis=0, keepdims=True) * (1.0 / members)
    moved = product(weights, cells - centre)
    common = centre + moved[members : members + 1]
    common_high, common_low = halves(
        jnp.concatenate([common[:, r * LANES : (r + 1) * LANES] for r in range(rows)], 0)
    )
    for part in range(members // share):
        for r in range(rows):
            for k in range(2):
                at = k * (members // 2) + part * half
                out[0, part, pl.ds(r * share + k * half, half)] = moved[
                    at : at + half, r * LANES : (r + 1) * LANES
                ].astype(BF16)
        out[0, part, rows * share : rows * share + rows] = common_high
        out[0, part, rows * share + rows :] = common_low


def apply_transform(share, begin, rows, states, inner, outer):
    blocks = states[0].shape[0]
    members = sum(piece.shape[1] for piece in states)
    lines = rows * (share + 2)
    return pl.pallas_call(
        partial(apply_kernel, share, begin, len(states)),
        grid=(blocks,),
        in_specs=[
            *[
                pl.BlockSpec((1, piece.shape[1], rows * LANES), lambda i: (i, 0, begin))
                for piece in states
            ],
            pl.BlockSpec(
                (1, members + 8, members), lambda i: (jnp.clip(i - 1, 0, blocks - 3), 0, 0)
            ),
            pl.BlockSpec((1, members + 8, members), lambda i: (i // (blocks - 1), 0, 0)),
        ],
        out_specs=pl.BlockSpec((1, members // share, lines, LANES), lambda i: (i, 0, 0, 0)),
        out_shape=jax.ShapeDtypeStruct((blocks, members // share, lines, LANES), BF16),
        name="apply",
    )(*states, inner, outer)


def unpack_kernel(share, rows, *refs):
    *chunks, out, stage = refs
    for part in range(PLANE):
        cols = slice(part * LANES, (part + 1) * LANES)
        for half, chunk in enumerate(chunks):
            common = chunk[part, 0, rows * share :].astype(F32)
            common = common[:rows] + common[rows:]
            for r in range(rows):
                field = chunk[part, 0, r * share : (r + 1) * share].astype(F32) + common[r : r + 1]
                for k in range(share // 8):
                    stage[part, pl.ds(64 * k + half * rows + r, 8, stride=8)] = field[
                        8 * k : 8 * k + 8
                    ]
        out[:, cols] = stage[part]


def unpack(share, rows, chunks):
    _, groups, lines, _ = chunks[0].shape
    return pl.pallas_call(
        partial(unpack_kernel, share, rows),
        grid=(groups,),
        in_specs=[pl.BlockSpec((PLANE, 1, lines, LANES), lambda i: (0, i, 0, 0))] * len(chunks),
        out_specs=pl.BlockSpec((share * ROWS, PLANE * LANES), lambda i: (0, i)),
        out_shape=jax.ShapeDtypeStruct((share * ROWS, groups * PLANE * LANES), F32),
        scratch_shapes=[pltpu.VMEM((PLANE, share * ROWS, LANES), F32)],
        name="unpack",
    )(*chunks)


def local(prior, drive, value, index, weight):
    members, rows, cols = prior.shape
    groups = lax.axis_size("member")
    planes = lax.axis_size("y")
    plane = lax.axis_index("y")
    upward = [(i + 1, i) for i in range(planes - 1)]
    downward = [(i, i + 1) for i in range(planes - 1)]
    me = lax.axis_index("member").reshape(1).astype(jnp.int32)
    inside = jnp.stack([plane > 0, plane < planes - 1]).astype(F32)
    axes = ("zc", "member")
    tied = lax.optimization_barrier
    extra = pack_extra(me, cols, drive, value, index, weight)
    prior, extra = tied((prior, extra))
    extra = lax.all_to_all(extra, "zc", 0, 0, tiled=True)
    early, extra = tied((pack(prior, 0), extra))
    early = lax.all_to_all(early, axes, 0, 0, tiled=True)
    late = lax.all_to_all(pack(prior, 1), axes, 0, 0, tiled=True)
    drive_bottom = lax.ppermute(extra[0], "y", upward)
    drive_top = lax.ppermute(extra[PLANE - 1], "y", downward)

    def around(chunk):
        cells = chunk.reshape(PLANE, groups, ROWS + 1, members // 2, LANES)
        bottom = lax.ppermute(cells[0], "y", upward)
        top = lax.ppermute(cells[PLANE - 1], "y", downward)
        return inside, cells, top, bottom, extra, drive_top, drive_bottom

    fields = around(early)
    first = forecast(*fields, 0, groups // 2)
    late, first = tied((late, first))
    later = around(late)
    second = forecast(*fields, groups // 2, groups)
    third = forecast(*later, 0, groups)
    states = (first, second, third)
    own, up, down = curvatures(states, extra)
    from_below = lax.ppermute(up, "y", upward)
    from_above = lax.ppermute(down, "y", downward)
    inner = transforms(own)
    outer = transforms(own, from_above, from_below)
    half = ROWS // 2
    chunks = []
    for begin in range(2):
        analysed = apply_transform(members, begin, half, states, inner, outer)
        sent = analysed.reshape(PLANE * groups, *analysed.shape[2:])
        chunks.append(lax.all_to_all(sent, axes, 0, 0, tiled=True).reshape(analysed.shape))
    return unpack(members, half, chunks).reshape(members, rows, cols)


def solution(mesh):
    groups, spaces = mesh.devices.shape
    fine = Mesh(mesh.devices.reshape(groups, spaces // PLANE, PLANE), ("member", "y", "zc"))
    rows = ("y", "zc")
    return jax.shard_map(
        local,
        mesh=fine,
        in_specs=(
            P("member", rows, None),
            P(rows, None),
            P(rows, "member", None),
            P(rows, "member", None),
            P(rows, "member", None),
        ),
        out_specs=P("member", rows, None),
        check_vma=False,
    )
```

```python
import math
from functools import partial

import jax
import jax.numpy as jnp
from jax import lax
from jax.experimental import pallas as pl
from jax.experimental.pallas import tpu as pltpu
from jax.sharding import Mesh, PartitionSpec as P


STEPS = 8
ITERS = 6
ROWS = 8
LANES = 128
PLANE = 4
F32 = jnp.float32
BF16 = jnp.bfloat16


def lane_index(rows):
    return lax.broadcasted_iota(jnp.int32, (rows, LANES), 1)


def halves(x):
    high = x.astype(BF16)
    return high, (x - high.astype(F32)).astype(BF16)


def thirds(x):
    high = x.astype(BF16)
    rest = x - high.astype(F32)
    mid = rest.astype(BF16)
    return high, mid, (rest - mid.astype(F32)).astype(BF16)


def product(a, b):
    ah, al = halves(a)
    bh, bl = halves(b)
    return jnp.dot(
        jnp.concatenate([ah, ah, al], 1),
        jnp.concatenate([bh, bl, bh], 0),
        preferred_element_type=F32,
    )


def against_rows(a, b):
    return lax.dot_general(a, b, (((1,), (1,)), ((), ())), preferred_element_type=F32)


def pack_kernel(tiles, prior, chunk, stage):
    lane = lane_index(16)
    groups = tiles // PLANE

    def place(tile):
        return lax.rem(tile, PLANE) * groups + tile // PLANE

    def rounding(tile, carry):
        cols = pl.ds(pl.multiple_of(tile * LANES, LANES), LANES)
        left = [jnp.zeros((16, LANES), F32)] * 2
        slot = lax.rem(tile, 2)
        stage[slot] = prior[:, cols]
        for row in range(ROWS):
            cells = jnp.concatenate(
                [stage[slot, pl.ds(row, 8, stride=8)], stage[slot, pl.ds(64 + row, 8, stride=8)]], 0
            )
            wanted = cells + left[row % 2]
            kept = wanted.astype(BF16)
            left[row % 2] = wanted - kept.astype(F32)
            chunk[place(tile), row] = kept
        return carry

    lax.fori_loop(0, tiles, rounding, 0)

    def edges(tile, carry):
        before = place(lax.rem(tile + tiles - 1, tiles))
        after = place(lax.rem(tile + 1, tiles))
        total = jnp.zeros((16, LANES), F32)
        for row in range(ROWS):
            both = jnp.where(
                lane >= LANES // 2, chunk[before, row].astype(F32), chunk[after, row].astype(F32)
            )
            moved = pltpu.roll(both, (16 * row + 8) % LANES, 1)
            total = jnp.where(lane // 16 == row, moved, total)
        chunk[place(tile), ROWS] = total.astype(BF16)
        return carry

    lax.fori_loop(0, tiles, edges, 0)


def extra_kernel(tiles, me_ref, drive, value, index, weight, extra):
    lane8 = lane_index(8)
    weights = weight[0].astype(F32)
    slot4 = lax.broadcasted_iota(jnp.int32, weights.shape, 0)
    for ahead in range(PLANE):
        part = lax.rem(me_ref[1] + ahead, PLANE)
        tile = me_ref[0] * PLANE + part

        def forcing(t):
            return drive[:, pl.ds(pl.multiple_of(lax.rem(t + tiles, tiles) * LANES, LANES), LANES)]

        main = forcing(tile)
        low = pltpu.roll(jnp.where(lane8 >= LANES // 2, forcing(tile - 1), main), 8, 1)
        low = jnp.where(lane8 < 32, low, 0.0)
        high = pltpu.roll(jnp.where(lane8 < LANES // 2, forcing(tile + 1), main), 8, 1)
        high = jnp.where((lane8 < 24) | (lane8 >= 120), high, 0.0)
        low = low + pltpu.roll(low, 32, 1)
        low = low + pltpu.roll(low, 64, 1)
        high = high + pltpu.roll(high, 32, 1)
        high = high + pltpu.roll(high, 64, 1)
        chosen = slot4 == part
        for slot, field in ((0, value[0]), (1, index[0].astype(F32)), (2, weights)):
            line = jnp.sum(jnp.where(chosen, field, 0.0), axis=0, keepdims=True)
            extra[ahead, slot : slot + 1, :] = line
        for slot, field in ((3, main), (4, low), (5, high)):
            for row in range(ROWS):
                extra[ahead, slot : slot + 1, row * LANES : (row + 1) * LANES] = field[row : row + 1]
        extra[ahead, 6:8, :] = jnp.zeros((2, ROWS * LANES), F32)


def pack_extra(me, cols, drive, value, index, weight):
    return pl.pallas_call(
        partial(extra_kernel, cols // LANES),
        in_specs=[pl.BlockSpec(memory_space=pltpu.SMEM)]
        + [pl.BlockSpec(memory_space=pltpu.VMEM)] * 4,
        out_shape=jax.ShapeDtypeStruct((PLANE, 8, ROWS * LANES), F32),
        name="pack_extra",
    )(me, drive, value, index, weight)


def pack(prior, half):
    members, rows, cols = prior.shape
    tiles = cols // LANES
    part = members // 2
    return pl.pallas_call(
        partial(pack_kernel, tiles),
        grid=(1,),
        in_specs=[pl.BlockSpec((part * rows, cols), lambda i: (half, 0))],
        out_specs=pl.BlockSpec((tiles, ROWS + 1, part, LANES), lambda i: (0, 0, 0, 0)),
        out_shape=jax.ShapeDtypeStruct((tiles, ROWS + 1, part, LANES), BF16),
        scratch_shapes=[pltpu.VMEM((2, part * rows, LANES), F32)],
        name="pack",
    )(prior.reshape(members * rows, cols))


def force_kernel(me_ref, own, one, two, three, extra, force, halo):
    for behind, came in enumerate((own, one, two, three)):
        strip = lax.rem(me_ref[1] + PLANE - behind, PLANE)
        extra[strip] = came[:8]
        halo[strip] = came[8:]
    for row in range((PLANE + 2) * ROWS):
        strip, r = divmod(row, ROWS)
        if strip == 0:
            source = halo.at[PLANE - 1]
        elif strip == PLANE + 1:
            source = halo.at[0]
        else:
            source = extra.at[strip - 1]
        for slot in range(3):
            line = source[3 + slot : 4 + slot, r * LANES : (r + 1) * LANES]
            force[slot, row] = jnp.broadcast_to(line * 0.005, (8, LANES))


def forcing(me, pieces):
    width = pieces[0].shape[1]
    return pl.pallas_call(
        force_kernel,
        in_specs=[pl.BlockSpec(memory_space=pltpu.SMEM)]
        + [pl.BlockSpec(memory_space=pltpu.VMEM)] * PLANE,
        out_shape=[
            jax.ShapeDtypeStruct((PLANE, 8, width), F32),
            jax.ShapeDtypeStruct((3, (PLANE + 2) * ROWS, 8, LANES), F32),
        ],
        scratch_shapes=[pltpu.VMEM((PLANE, 8, width), F32)],
        name="forcing",
    )(me, *pieces)


def forecast_kernel(inside, cells, top, bottom, force, out, state):
    depth = (PLANE + 2) * ROWS
    lane = lane_index(8)

    for row in range(depth):
        strip, r = divmod(row, ROWS)
        if strip == 0:
            source = top
        elif strip == PLANE + 1:
            source = bottom
        else:
            source = cells.at[strip - 1]
        main = jnp.concatenate([source[0, r], source[1, r]], 0).astype(F32) * 0.05
        edge = jnp.concatenate([source[0, ROWS], source[1, ROWS]], 0).astype(F32) * 0.05
        low = jnp.zeros((8, LANES), F32)
        high = jnp.zeros((8, LANES), F32)
        for k in range(4):
            here = main[8 * k : 8 * k + 8]
            state[k, row] = here
            moved = pltpu.roll(here, 32 * k + 8, 1)
            beside = pltpu.roll(edge[8 * k : 8 * k + 8], (32 * k - 16 * r) % LANES, 1)
            at = (lane - 32 * k + LANES) % LANES
            low = jnp.where(at < 8, beside, jnp.where(at < 24, moved, low))
            high = jnp.where(
                (at < 8) | (at >= 120), moved, jnp.where(at < 16, beside, high)
            )
        state[4, row] = low
        state[5, row] = high

    keep_top, keep_bottom = inside[0], inside[1]

    def group(g, carry):
        kind = jnp.maximum(g - 3, 0)
        for step in range(STEPS):
            first, last = step + 1, depth - 2 - step
            above, here = state[g, first - 1], state[g, first]
            for row in range(first, last + 1):
                below = state[g, row + 1]
                east, west = pltpu.roll(here, LANES - 1, 1), pltpu.roll(here, 1, 1)
                turn = (west - east) + (above - below) + 0.05
                fresh = (
                    force[kind, row]
                    + here * turn
                    + 0.05 * (east + west)
                    + 0.4 * (above + below)
                )
                if row < ROWS:
                    fresh = fresh * keep_top
                if row >= depth - ROWS:
                    fresh = fresh * keep_bottom
                state[g, row] = fresh
                above, here = here, below
        return carry

    lax.fori_loop(0, 6, group, 0)

    outer = (lane < 8) | (lane >= LANES - 8)
    for row in range(ROWS, depth - ROWS):
        strip, r = divmod(row - ROWS, ROWS)
        both = jnp.where(lane % 32 < 8, state[5, row], state[4, row])
        for k in range(4):
            side = pltpu.roll(both, (120 - 32 * k) % LANES, 1)
            out[strip, 8 * k : 8 * k + 8, r * LANES : (r + 1) * LANES] = 20.0 * jnp.where(
                outer, side, state[k, row]
            )


def forecast(inside, cells, top, bottom, force, begin, end):
    _, _, lines, members, _ = cells.shape
    at = begin // 2
    whole = lambda shape: pl.BlockSpec(shape, lambda i: (0,) * len(shape))
    return pl.pallas_call(
        forecast_kernel,
        grid=((end - begin) // 2,),
        in_specs=[
            pl.BlockSpec(memory_space=pltpu.SMEM),
            pl.BlockSpec((PLANE, 2, lines, members, LANES), lambda i: (0, i + at, 0, 0, 0)),
            pl.BlockSpec((2, lines, members, LANES), lambda i: (i + at, 0, 0, 0)),
            pl.BlockSpec((2, lines, members, LANES), lambda i: (i + at, 0, 0, 0)),
            whole(force.shape),
        ],
        out_specs=pl.BlockSpec((PLANE, 2 * members, ROWS * LANES), lambda i: (0, i, 0)),
        out_shape=jax.ShapeDtypeStruct((PLANE, (end - begin) * members, ROWS * LANES), F32),
        scratch_shapes=[
            pltpu.VMEM((6, (PLANE + 2) * ROWS, 8, LANES), F32),
        ],
        name="forecast",
    )(inside, cells, top, bottom, force)


def to_tile(line):
    return jnp.concatenate([line[:, r * LANES : (r + 1) * LANES] for r in range(ROWS)], 0)


def to_line(tile):
    return jnp.concatenate([tile[r : r + 1] for r in range(ROWS)], 1)


def curvature_kernel(pieces, *refs):
    states, (obs, own, up, down) = refs[:pieces], refs[pieces:]
    block = pl.program_id(0)
    blocks = pl.num_programs(0)
    cells = jnp.concatenate([piece[0] for piece in states], 0)
    members = cells.shape[0]
    centre = jnp.sum(cells, axis=0, keepdims=True) * (1.0 / members)
    anomaly = (cells - centre).astype(BF16)
    value, index, weight = obs[0, 0:1], obs[0, 1:2], obs[0, 2:3]
    row_of = jnp.floor(index * (1.0 / LANES))
    col_of = index - row_of * LANES
    count = index.shape[1]
    in_row = lax.broadcasted_iota(jnp.int32, (ROWS, count), 0).astype(F32) == row_of
    in_col = jnp.where(
        lax.broadcasted_iota(jnp.int32, (LANES, count), 0).astype(F32) == col_of, 1.0, 0.0
    ).astype(BF16)
    parts = jnp.concatenate(thirds(to_tile(centre)), 0)
    seen = jnp.dot(parts, in_col, preferred_element_type=F32)
    seen = (seen[:ROWS] + seen[ROWS : 2 * ROWS]) + seen[2 * ROWS :]
    obs_mean = jnp.sum(jnp.where(in_row, seen, 0.0), axis=0, keepdims=True)
    innovation = (value - obs_mean).astype(BF16).astype(F32)
    pull_high, pull_low = halves(weight * innovation)
    spread = jnp.concatenate(
        [
            jnp.where(in_row, weight, 0.0),
            jnp.where(in_row, pull_high.astype(F32), 0.0),
            jnp.where(in_row, pull_low.astype(F32), 0.0),
        ],
        0,
    ).astype(BF16)
    summed = against_rows(spread, in_col)
    weights = summed[:ROWS]
    pulls = summed[ROWS : 2 * ROWS] + summed[2 * ROWS :]
    row_pos = lax.broadcasted_iota(jnp.int32, (ROWS, LANES), 0).astype(F32)
    span = float(ROWS)
    fall_down = jnp.exp(-2.0 * (span - row_pos) * (span - row_pos) / (span * span))
    fall_up = jnp.exp(-2.0 * (row_pos + 1.0) * (row_pos + 1.0) / (span * span))
    wide = anomaly.astype(F32)
    ones = jnp.ones((ROWS, LANES), F32)
    factors = (ones, fall_up, fall_down)
    terms = [
        against_rows((wide * to_line(weights * f)).astype(BF16), anomaly) for f in factors
    ]
    lines = []
    for f in factors:
        lines.extend(thirds(to_line(pulls * f)))
    lines.append(jnp.zeros((7, count), BF16))
    vectors = against_rows(jnp.concatenate(lines, 0), anomaly)
    sides = [
        (vectors[3 * i : 3 * i + 1] + vectors[3 * i + 1 : 3 * i + 2]) + vectors[3 * i + 2 : 3 * i + 3]
        for i in range(3)
    ]
    pad = jnp.zeros((7, members), F32)

    @pl.when(block == 0)
    def _():
        own[...] = jnp.zeros_like(own)
        up[:members] = terms[1]
        up[members:] = jnp.concatenate([sides[1], pad], 0)

    own[block, :members] += terms[0]
    own[block, members:] += jnp.concatenate([sides[0], pad], 0)

    @pl.when(block > 0)
    def _():
        own[block - 1, :members] += terms[1]
        own[block - 1, members:] += jnp.concatenate([sides[1], pad], 0)

    @pl.when(block < blocks - 1)
    def _():
        own[block + 1, :members] += terms[2]
        own[block + 1, members:] += jnp.concatenate([sides[2], pad], 0)

    @pl.when(block == blocks - 1)
    def _():
        down[:members] = terms[2]
        down[members:] = jnp.concatenate([sides[2], pad], 0)


def of_block(states):
    return [pl.BlockSpec((1, *piece.shape[1:]), lambda i: (i, 0, 0)) for piece in states]


def curvatures(states, obs):
    blocks, _, width = states[0].shape
    members = sum(piece.shape[1] for piece in states)
    whole = lambda shape: pl.BlockSpec(shape, lambda i: (0,) * len(shape))
    return pl.pallas_call(
        partial(curvature_kernel, len(states)),
        grid=(blocks,),
        in_specs=[*of_block(states), pl.BlockSpec((1, 8, width), lambda i: (i, 0, 0))],
        out_specs=[
            whole((blocks, members + 8, members)),
            whole((members + 8, members)),
            whole((members + 8, members)),
        ],
        out_shape=[
            jax.ShapeDtypeStruct((blocks, members + 8, members), F32),
            jax.ShapeDtypeStruct((members + 8, members), F32),
            jax.ShapeDtypeStruct((members + 8, members), F32),
        ],
        name="curvature",
    )(*states, obs)


def transform_kernel(edges, *refs):
    own, *rest = refs
    *halo, out, iterate, inverse = rest
    blocks, size, _ = iterate.shape
    row = lax.broadcasted_iota(jnp.int32, (size, size), 0)
    col = lax.broadcasted_iota(jnp.int32, (size, size), 1)
    diagonal = row == col

    def middle_of(x):
        return jnp.where(diagonal, 1.5 - 0.5 * x, -0.5 * x)

    norms, sides = [], []
    for b in range(blocks):
        place = b * (own.shape[0] - 1) if edges else b + 1
        matrix, side = own[place, :size], own[place, size:]
        if edges:
            matrix, side = matrix + halo[b][:size], side + halo[b][size:]
        matrix = matrix + jnp.where(diagonal, size - 1.0, 0.0)
        squares = jnp.sum(jnp.sum(matrix * matrix, axis=0, keepdims=True), axis=1, keepdims=True)
        norm = jnp.sqrt(squares)
        start = matrix / norm
        middle = middle_of(start)
        inverse[b] = middle
        iterate[b] = product(start, middle)
        norms.append(norm)
        sides.append(side)

    def sweep(i, carry):
        middles = [middle_of(product(inverse[b], iterate[b])) for b in range(blocks)]
        for b in range(blocks):
            both = product(jnp.concatenate([iterate[b], inverse[b]], 0), middles[b])
            iterate[b] = both[:size]
            inverse[b] = both[size:]
        return carry

    lax.fori_loop(0, ITERS - 2, sweep, 0)
    middles = [middle_of(product(inverse[b], iterate[b])) for b in range(blocks)]
    finals = [product(inverse[b], middles[b]) for b in range(blocks)]
    for b in range(blocks):
        flipped = finals[b].T
        inner = product(sides[b], flipped)
        shift = product(inner, flipped) / norms[b]
        out[b, :size] = flipped * (math.sqrt(size - 1.0) / jnp.sqrt(norms[b]))
        out[b, size:] = shift


def transforms(own, *halo):
    total, lines, size = own.shape
    blocks = len(halo) or total - 2
    return pl.pallas_call(
        partial(transform_kernel, bool(halo)),
        out_shape=jax.ShapeDtypeStruct((blocks, lines, size), F32),
        scratch_shapes=[
            pltpu.VMEM((blocks, size, size), F32),
            pltpu.VMEM((blocks, size, size), F32),
        ],
        name="transform",
    )(own, *halo)


def apply_kernel(share, pieces, *refs):
    states, (inner, outer, out) = refs[:pieces], refs[pieces:]
    block = pl.program_id(0)
    within = (block > 0) & (block < pl.num_programs(0) - 1)
    cells = jnp.concatenate([piece[0] for piece in states], 0)
    members, width = cells.shape
    rows = width // LANES
    half = share // 2
    weights = jnp.where(within, inner[0], outer[0])
    centre = jnp.sum(cells, axis=0, keepdims=True) * (1.0 / members)
    moved = product(weights, cells - centre)
    common = centre + moved[members : members + 1]
    common_high, common_low = halves(
        jnp.concatenate([common[:, r * LANES : (r + 1) * LANES] for r in range(rows)], 0)
    )
    for part in range(members // share):
        for r in range(rows):
            for k in range(2):
                at = k * (members // 2) + part * half
                out[0, part, pl.ds(r * share + k * half, half)] = moved[
                    at : at + half, r * LANES : (r + 1) * LANES
                ].astype(BF16)
        out[0, part, rows * share : rows * share + rows] = common_high
        out[0, part, rows * share + rows :] = common_low


def apply_transform(share, begin, rows, states, inner, outer):
    blocks = states[0].shape[0]
    members = sum(piece.shape[1] for piece in states)
    lines = rows * (share + 2)
    return pl.pallas_call(
        partial(apply_kernel, share, len(states)),
        grid=(blocks,),
        in_specs=[
            *[
                pl.BlockSpec((1, piece.shape[1], rows * LANES), lambda i: (i, 0, begin))
                for piece in states
            ],
            pl.BlockSpec(
                (1, members + 8, members), lambda i: (jnp.clip(i - 1, 0, blocks - 3), 0, 0)
            ),
            pl.BlockSpec((1, members + 8, members), lambda i: (i // (blocks - 1), 0, 0)),
        ],
        out_specs=pl.BlockSpec((1, members // share, lines, LANES), lambda i: (i, 0, 0, 0)),
        out_shape=jax.ShapeDtypeStruct((blocks, members // share, lines, LANES), BF16),
        name="apply",
    )(*states, inner, outer)


def unpack_kernel(share, rows, *refs):
    *chunks, out, stage = refs
    for part in range(PLANE):
        cols = slice(part * LANES, (part + 1) * LANES)
        for half, chunk in enumerate(chunks):
            common = chunk[part, 0, rows * share :].astype(F32)
            common = common[:rows] + common[rows:]
            for r in range(rows):
                field = chunk[part, 0, r * share : (r + 1) * share].astype(F32) + common[r : r + 1]
                for k in range(share // 8):
                    stage[part, pl.ds(64 * k + half * rows + r, 8, stride=8)] = field[
                        8 * k : 8 * k + 8
                    ]
        out[:, cols] = stage[part]


def unpack(share, rows, chunks):
    _, groups, lines, _ = chunks[0].shape
    return pl.pallas_call(
        partial(unpack_kernel, share, rows),
        grid=(groups,),
        in_specs=[pl.BlockSpec((PLANE, 1, lines, LANES), lambda i: (0, i, 0, 0))] * len(chunks),
        out_specs=pl.BlockSpec((share * ROWS, PLANE * LANES), lambda i: (0, i)),
        out_shape=jax.ShapeDtypeStruct((share * ROWS, groups * PLANE * LANES), F32),
        scratch_shapes=[pltpu.VMEM((PLANE, share * ROWS, LANES), F32)],
        name="unpack",
    )(*chunks)


def local(prior, drive, value, index, weight):
    members, rows, cols = prior.shape
    groups = lax.axis_size("member")
    planes = lax.axis_size("y")
    plane = lax.axis_index("y")
    upward = [(i + 1, i) for i in range(planes - 1)]
    downward = [(i, i + 1) for i in range(planes - 1)]
    me = jnp.stack([lax.axis_index("member"), lax.axis_index("zc")]).astype(jnp.int32)
    inside = jnp.stack([plane > 0, plane < planes - 1]).astype(F32)
    axes = ("zc", "member")
    tied = lax.optimization_barrier
    early, drive = tied((pack(prior, 0), drive))
    outward = [
        (PLANE * i + edge, PLANE * j + edge)
        for edge, pairs in ((0, upward), (PLANE - 1, downward))
        for i, j in pairs
    ]
    extra = pack_extra(me, cols, drive, value, index, weight)
    outer_rows = lax.ppermute(extra, ("y", "zc"), outward)
    pieces = [jnp.concatenate([extra[d], outer_rows[d]], 0) for d in range(PLANE)]
    for d in range(1, PLANE):
        pieces[d] = lax.ppermute(
            pieces[d], "zc", [(i, (i + d) % PLANE) for i in range(PLANE)]
        )
    extra, force = forcing(me, pieces)
    early = lax.all_to_all(early, axes, 0, 0, tiled=True)
    late = pack(prior, 1)
    late = lax.all_to_all(late, axes, 0, 0, tiled=True)

    def around(chunk):
        cells = chunk.reshape(PLANE, groups, ROWS + 1, members // 2, LANES)
        bottom = lax.ppermute(cells[0], "y", upward)
        top = lax.ppermute(cells[PLANE - 1], "y", downward)
        return inside, cells, top, bottom, force

    fields = around(early)
    first = forecast(*fields, 0, groups // 2)
    late, first = tied((late, first))
    later = around(late)
    second = forecast(*fields, groups // 2, groups)
    third = forecast(*later, 0, groups)
    states = (first, second, third)
    own, up, down = curvatures(states, extra)
    from_below = lax.ppermute(up, "y", upward)
    from_above = lax.ppermute(down, "y", downward)
    inner = transforms(own)
    outer = transforms(own, from_above, from_below)
    analysed = apply_transform(members, 0, ROWS, states, inner, outer)
    sent = analysed.reshape(PLANE * groups, *analysed.shape[2:])
    back = lax.all_to_all(sent, axes, 0, 0, tiled=True).reshape(analysed.shape)
    return unpack(members, ROWS, [back]).reshape(members, rows, cols)


def solution(mesh):
    groups, spaces = mesh.devices.shape
    fine = Mesh(mesh.devices.reshape(groups, spaces // PLANE, PLANE), ("member", "y", "zc"))
    rows = ("y", "zc")
    return jax.shard_map(
        local,
        mesh=fine,
        in_specs=(
            P("member", rows, None),
            P(rows, None),
            P(rows, "member", None),
            P(rows, "member", None),
            P(rows, "member", None),
        ),
        out_specs=P("member", rows, None),
        check_vma=False,
    )
```

```python
import math
from functools import partial

import jax
import jax.numpy as jnp
from jax import lax
from jax.experimental import pallas as pl
from jax.experimental.pallas import tpu as pltpu
from jax.sharding import Mesh, PartitionSpec as P


STEPS = 8
ITERS = 6
ROWS = 8
LANES = 128
PLANE = 4
F32 = jnp.float32
BF16 = jnp.bfloat16


def lane_index(rows):
    return lax.broadcasted_iota(jnp.int32, (rows, LANES), 1)


def halves(x):
    high = x.astype(BF16)
    return high, (x - high.astype(F32)).astype(BF16)


def thirds(x):
    high = x.astype(BF16)
    rest = x - high.astype(F32)
    mid = rest.astype(BF16)
    return high, mid, (rest - mid.astype(F32)).astype(BF16)


def product(a, b):
    ah, al = halves(a)
    bh, bl = halves(b)
    return jnp.dot(
        jnp.concatenate([ah, ah, al], 1),
        jnp.concatenate([bh, bl, bh], 0),
        preferred_element_type=F32,
    )


def against_rows(a, b):
    return lax.dot_general(a, b, (((1,), (1,)), ((), ())), preferred_element_type=F32)


def to_tile(line):
    return jnp.concatenate([line[:, r * LANES : (r + 1) * LANES] for r in range(ROWS)], 0)


def to_line(tile):
    return jnp.concatenate([tile[r : r + 1] for r in range(ROWS)], 1)


def pack_kernel(tiles, prior, chunk, stage):
    lane = lane_index(16)
    groups = tiles // PLANE

    def place(tile):
        return lax.rem(tile, PLANE) * groups + tile // PLANE

    def rounding(tile, carry):
        cols = pl.ds(pl.multiple_of(tile * LANES, LANES), LANES)
        left = [jnp.zeros((16, LANES), F32)] * 2
        slot = lax.rem(tile, 4)
        stage[slot] = prior[:, cols]
        for row in range(ROWS):
            cells = jnp.concatenate(
                [stage[slot, pl.ds(row, 8, stride=8)], stage[slot, pl.ds(64 + row, 8, stride=8)]], 0
            )
            wanted = cells + left[row % 2]
            kept = wanted.astype(BF16)
            left[row % 2] = wanted - kept.astype(F32)
            chunk[place(tile), row] = kept
        return carry

    lax.fori_loop(0, tiles, rounding, 0, unroll=4)

    def edges(tile, carry):
        before = place(lax.rem(tile + tiles - 1, tiles))
        after = place(lax.rem(tile + 1, tiles))
        total = jnp.zeros((16, LANES), F32)
        for row in range(ROWS):
            both = jnp.where(
                lane >= LANES // 2, chunk[before, row].astype(F32), chunk[after, row].astype(F32)
            )
            moved = pltpu.roll(both, (16 * row + 8) % LANES, 1)
            total = jnp.where(lane // 16 == row, moved, total)
        chunk[place(tile), ROWS] = total.astype(BF16)
        return carry

    lax.fori_loop(0, tiles, edges, 0, unroll=4)


def extra_kernel(tiles, me_ref, drive, value, index, weight, extra):
    lane8 = lane_index(8)
    weights = weight[0].astype(F32)
    slot4 = lax.broadcasted_iota(jnp.int32, weights.shape, 0)
    for ahead in range(PLANE):
        part = lax.rem(me_ref[1] + ahead, PLANE)
        tile = me_ref[0] * PLANE + part

        def forcing(t):
            return drive[:, pl.ds(pl.multiple_of(lax.rem(t + tiles, tiles) * LANES, LANES), LANES)]

        main = forcing(tile)
        both = jnp.where(lane8 >= LANES // 2, forcing(tile - 1), forcing(tile + 1))
        chosen = slot4 == part
        for slot, field in ((0, value[0]), (1, index[0].astype(F32)), (2, weights)):
            line = jnp.sum(jnp.where(chosen, field, 0.0), axis=0, keepdims=True)
            extra[ahead, slot : slot + 1, :] = line
        extra[ahead, 5:8, :] = jnp.zeros((3, ROWS * LANES), F32)
        for slot, field in ((3, main), (4, both)):
            for row in range(ROWS):
                extra[ahead, slot : slot + 1, row * LANES : (row + 1) * LANES] = field[row : row + 1]


def pack_extra(me, cols, drive, value, index, weight):
    return pl.pallas_call(
        partial(extra_kernel, cols // LANES),
        in_specs=[pl.BlockSpec(memory_space=pltpu.SMEM)]
        + [pl.BlockSpec(memory_space=pltpu.VMEM)] * 4,
        out_shape=jax.ShapeDtypeStruct((PLANE, 8, ROWS * LANES), F32),
        name="pack_extra",
        compiler_params=pltpu.CompilerParams(vmem_limit_bytes=8 << 20),
    )(me, drive, value, index, weight)


def pack(prior):
    members, rows, cols = prior.shape
    tiles = cols // LANES
    part = members // 2
    return pl.pallas_call(
        partial(pack_kernel, tiles),
        grid=(2,),
        in_specs=[pl.BlockSpec((part * rows, cols), lambda i: (i, 0))],
        out_specs=pl.BlockSpec((tiles, ROWS + 1, part, LANES), lambda i: (0, 0, i, 0)),
        out_shape=jax.ShapeDtypeStruct((tiles, ROWS + 1, members, LANES), BF16),
        scratch_shapes=[pltpu.VMEM((4, part * rows, LANES), F32)],
        name="pack",
    )(prior.reshape(members * rows, cols))


def force_kernel(me_ref, own, one, two, three, extra, force, halo):
    for behind, came in enumerate((own, one, two, three)):
        strip = lax.rem(me_ref[1] + PLANE - behind, PLANE)
        extra[strip] = came[:8]
        halo[strip] = came[8:]
    lane = lane_index(8)
    for strip in range(PLANE + 2):
        if strip == 0:
            source = halo.at[PLANE - 1]
        elif strip == PLANE + 1:
            source = halo.at[0]
        else:
            source = extra.at[strip - 1]
        main = to_tile(source[3:4]) * 0.005
        both = to_tile(source[4:5]) * 0.005
        for b in range(8):
            line = pltpu.roll(main, (LANES + 8 - 32 * (b % 4)) % LANES, 1)
            if b % 4 == 0:
                line = jnp.where(lane < 8, pltpu.roll(both, 8, 1), line)
            if b % 4 == 3:
                line = jnp.where(lane >= 40, pltpu.roll(both, 40, 1), line)
            force[pl.ds(strip * 8 * ROWS + b, 8, stride=8)] = line


def forcing(me, pieces):
    width = pieces[0].shape[1]
    return pl.pallas_call(
        force_kernel,
        in_specs=[pl.BlockSpec(memory_space=pltpu.SMEM)]
        + [pl.BlockSpec(memory_space=pltpu.VMEM)] * PLANE,
        out_shape=[
            jax.ShapeDtypeStruct((PLANE, 8, width), F32),
            jax.ShapeDtypeStruct(((PLANE + 2) * ROWS * 8, LANES), F32),
        ],
        scratch_shapes=[pltpu.VMEM((PLANE, 8, width), F32)],
        name="forcing",
        compiler_params=pltpu.CompilerParams(vmem_limit_bytes=8 << 20),
    )(me, *pieces)


def forecast_kernel(
    inside, cells, top, bottom, force, out, now, later, push, turned, stage, done
):
    depth, span = now.shape[:2]
    lane = lane_index(LANES)
    unit = jnp.where(lax.broadcasted_iota(jnp.int32, lane.shape, 0) == lane, 1.0, 0.0).astype(BF16)
    line = lax.broadcasted_iota(jnp.int32, (8 * span, 2 * LANES), 0)
    sub = lax.rem(line, 8)
    wanted = 32 * lax.rem(sub, 4) + line // 8 - 8
    place = lax.broadcasted_iota(jnp.int32, line.shape, 1)
    spread = (lax.rem(place, LANES) == wanted) & (place // LANES == sub // 4)
    spread = jnp.where(spread, 1.0, 0.0).astype(BF16)

    for strip in range(PLANE + 2):
        if strip == 0:
            source = top
        elif strip == PLANE + 1:
            source = bottom
        else:
            source = cells.at[strip - 1]
        for h in range(2):
            edge = source[4 * h : 4 * h + 4, ROWS].reshape(LANES, LANES)
            turned[0, h * LANES : (h + 1) * LANES] = against_rows(unit, edge) * 0.05

        def load(i, carry):
            for k in range(4):
                r = 4 * i + k
                row = strip * ROWS + r
                both = jnp.concatenate(
                    [source[4 * h : 4 * h + 4, r].reshape(LANES, LANES) for h in range(2)], 1
                )
                main = against_rows(spread, both) * 0.05
                for c in range(span):
                    now[row, c] = main[8 * c : 8 * c + 8]
                at = pl.multiple_of(16 * r, 16)
                for h in range(2):
                    for c in range(8):
                        low = turned[0, pl.ds(h * LANES + at + c, 1)]
                        high = turned[0, pl.ds(h * LANES + at + 8 + c, 1)]
                        now[row, c, 4 * h : 4 * h + 1] = low
                        now[row, span - 8 + c, 4 * h + 3 : 4 * h + 4] = high
                pushes = force[pl.ds(pl.multiple_of(row * 8, 8), 8)]
                for c in range(span):
                    push[row, c] = jnp.broadcast_to(pushes[:, c : c + 1], (8, LANES))
            return carry

        lax.fori_loop(0, ROWS // 4, load, 0)

    keep_top, keep_bottom = inside[0], inside[1]
    source, target = now, later
    for step in range(STEPS):
        low, high = step + 1, span - 2 - step

        def pair(i, carry, source=source, target=target, low=low, high=high):
            row = low + 2 * i
            west = [source[row + k, low - 1] for k in range(2)]
            here = [source[row + k, low] for k in range(2)]
            for c in range(low, high + 1):
                east = [source[row + k, c + 1] for k in range(2)]
                column = [source[row - 1, c], *here, source[row + 2, c]]
                for k in range(2):
                    above, below = column[k], column[k + 2]
                    turn = (west[k] - east[k]) + (above - below) + 0.05
                    target[row + k, c] = (
                        push[row + k, c]
                        + here[k] * turn
                        + 0.05 * (east[k] + west[k])
                        + 0.4 * (above + below)
                    )
                west, here = here, east
            return carry

        lax.fori_loop(0, (depth - 2 - 2 * step) // 2, pair, 0)
        if step < STEPS - 1:
            for c in range(low, high + 1):
                target[ROWS - 1, c] = target[ROWS - 1, c] * keep_top
                target[depth - ROWS, c] = target[depth - ROWS, c] * keep_bottom
        source, target = target, source

    copies = []
    for strip in range(PLANE):

        def save(i, carry):
            for k in range(2):
                row = (strip + 1) * ROWS + 2 * i + k
                for c in range(span - 16):
                    turned[k, 8 * c : 8 * c + 8] = 20.0 * source[row, c + 8]
            for k in range(2):
                at = pl.multiple_of((2 * i + k) * LANES, LANES)
                for h in range(2):
                    columns = [
                        turned[k, pl.ds(64 * c + 4 * h + b, 8, stride=8)]
                        for b in range(4)
                        for c in range(4)
                    ]
                    part = slice(h * LANES, (h + 1) * LANES)
                    stage[strip, part, pl.ds(at, LANES)] = jnp.concatenate(columns, 0).T
            return carry

        lax.fori_loop(0, ROWS // 2, save, 0)
        copies.append(pltpu.make_async_copy(stage.at[strip], out.at[strip], done.at[strip]))
        copies[-1].start()
    for copy in copies:
        copy.wait()


def forecast(inside, cells, top, bottom, force):
    field = pltpu.VMEM(((PLANE + 2) * ROWS, 48, 8, LANES), F32)
    vmem = pl.BlockSpec(memory_space=pltpu.VMEM)
    return pl.pallas_call(
        forecast_kernel,
        in_specs=[pl.BlockSpec(memory_space=pltpu.SMEM), vmem, vmem, vmem, vmem],
        out_specs=pl.BlockSpec(memory_space=pl.ANY),
        out_shape=jax.ShapeDtypeStruct((PLANE, 2 * LANES, ROWS * LANES), F32),
        scratch_shapes=[
            field,
            field,
            field,
            pltpu.VMEM((2, 2 * LANES, LANES), F32),
            pltpu.VMEM((PLANE, 2 * LANES, ROWS * LANES), F32),
            pltpu.SemaphoreType.DMA((PLANE,)),
        ],
        name="forecast",
        compiler_params=pltpu.CompilerParams(vmem_limit_bytes=42 << 20),
    )(inside, cells, top, bottom, force)


def curvature_kernel(pieces, *refs):
    states, (obs, own, up, down) = refs[:pieces], refs[pieces:]
    block = pl.program_id(0)
    blocks = pl.num_programs(0)
    cells = jnp.concatenate([piece[0] for piece in states], 0)
    members = cells.shape[0]
    centre = jnp.sum(cells, axis=0, keepdims=True) * (1.0 / members)
    anomaly = (cells - centre).astype(BF16)
    value, index, weight = obs[0, 0:1], obs[0, 1:2], obs[0, 2:3]
    row_of = jnp.floor(index * (1.0 / LANES))
    col_of = index - row_of * LANES
    count = index.shape[1]
    in_row = lax.broadcasted_iota(jnp.int32, (ROWS, count), 0).astype(F32) == row_of
    in_col = jnp.where(
        lax.broadcasted_iota(jnp.int32, (LANES, count), 0).astype(F32) == col_of, 1.0, 0.0
    ).astype(BF16)
    parts = jnp.concatenate(thirds(to_tile(centre)), 0)
    seen = jnp.dot(parts, in_col, preferred_element_type=F32)
    seen = (seen[:ROWS] + seen[ROWS : 2 * ROWS]) + seen[2 * ROWS :]
    obs_mean = jnp.sum(jnp.where(in_row, seen, 0.0), axis=0, keepdims=True)
    innovation = (value - obs_mean).astype(BF16).astype(F32)
    pull_high, pull_low = halves(weight * innovation)
    spread = jnp.concatenate(
        [
            jnp.where(in_row, weight, 0.0),
            jnp.where(in_row, pull_high.astype(F32), 0.0),
            jnp.where(in_row, pull_low.astype(F32), 0.0),
        ],
        0,
    ).astype(BF16)
    summed = against_rows(spread, in_col)
    weights = summed[:ROWS]
    pulls = summed[ROWS : 2 * ROWS] + summed[2 * ROWS :]
    row_pos = lax.broadcasted_iota(jnp.int32, (ROWS, LANES), 0).astype(F32)
    span = float(ROWS)
    fall_down = jnp.exp(-2.0 * (span - row_pos) * (span - row_pos) / (span * span))
    fall_up = jnp.exp(-2.0 * (row_pos + 1.0) * (row_pos + 1.0) / (span * span))
    wide = anomaly.astype(F32)
    ones = jnp.ones((ROWS, LANES), F32)
    factors = (ones, fall_up, fall_down)
    terms = [
        against_rows((wide * to_line(weights * f)).astype(BF16), anomaly) for f in factors
    ]
    lines = []
    for f in factors:
        lines.extend(thirds(to_line(pulls * f)))
    lines.append(jnp.zeros((7, count), BF16))
    vectors = against_rows(jnp.concatenate(lines, 0), anomaly)
    sides = [
        (vectors[3 * i : 3 * i + 1] + vectors[3 * i + 1 : 3 * i + 2]) + vectors[3 * i + 2 : 3 * i + 3]
        for i in range(3)
    ]
    pad = jnp.zeros((7, members), F32)

    @pl.when(block == 0)
    def _():
        own[...] = jnp.zeros_like(own)
        up[:members] = terms[1]
        up[members:] = jnp.concatenate([sides[1], pad], 0)

    own[block, :members] += terms[0]
    own[block, members:] += jnp.concatenate([sides[0], pad], 0)

    @pl.when(block > 0)
    def _():
        own[block - 1, :members] += terms[1]
        own[block - 1, members:] += jnp.concatenate([sides[1], pad], 0)

    @pl.when(block < blocks - 1)
    def _():
        own[block + 1, :members] += terms[2]
        own[block + 1, members:] += jnp.concatenate([sides[2], pad], 0)

    @pl.when(block == blocks - 1)
    def _():
        down[:members] = terms[2]
        down[members:] = jnp.concatenate([sides[2], pad], 0)


def of_block(states):
    return [pl.BlockSpec((1, *piece.shape[1:]), lambda i: (i, 0, 0)) for piece in states]


def curvatures(states, obs):
    blocks, _, width = states[0].shape
    members = sum(piece.shape[1] for piece in states)
    whole = lambda shape: pl.BlockSpec(shape, lambda i: (0,) * len(shape))
    return pl.pallas_call(
        partial(curvature_kernel, len(states)),
        grid=(blocks,),
        in_specs=[*of_block(states), pl.BlockSpec((1, 8, width), lambda i: (i, 0, 0))],
        out_specs=[
            whole((blocks, members + 8, members)),
            whole((members + 8, members)),
            whole((members + 8, members)),
        ],
        out_shape=[
            jax.ShapeDtypeStruct((blocks, members + 8, members), F32),
            jax.ShapeDtypeStruct((members + 8, members), F32),
            jax.ShapeDtypeStruct((members + 8, members), F32),
        ],
        name="curvature",
        compiler_params=pltpu.CompilerParams(vmem_limit_bytes=16 << 20),
    )(*states, obs)


def transform_kernel(edges, *refs):
    own, *rest = refs
    *halo, out, iterate, inverse = rest
    blocks, size, _ = iterate.shape
    row = lax.broadcasted_iota(jnp.int32, (size, size), 0)
    col = lax.broadcasted_iota(jnp.int32, (size, size), 1)
    diagonal = row == col

    def middle_of(x):
        return jnp.where(diagonal, 1.5 - 0.5 * x, -0.5 * x)

    norms, sides = [], []
    for b in range(blocks):
        place = b * (own.shape[0] - 1) if edges else b + 1
        matrix, side = own[place, :size], own[place, size:]
        if edges:
            matrix, side = matrix + halo[b][:size], side + halo[b][size:]
        matrix = matrix + jnp.where(diagonal, size - 1.0, 0.0)
        squares = jnp.sum(jnp.sum(matrix * matrix, axis=0, keepdims=True), axis=1, keepdims=True)
        norm = jnp.sqrt(squares)
        start = matrix / norm
        middle = middle_of(start)
        inverse[b] = middle
        iterate[b] = product(start, middle)
        norms.append(norm)
        sides.append(side)

    def sweep(i, carry):
        middles = [middle_of(product(inverse[b], iterate[b])) for b in range(blocks)]
        for b in range(blocks):
            both = product(jnp.concatenate([iterate[b], inverse[b]], 0), middles[b])
            iterate[b] = both[:size]
            inverse[b] = both[size:]
        return carry

    lax.fori_loop(0, ITERS - 2, sweep, 0)
    middles = [middle_of(product(inverse[b], iterate[b])) for b in range(blocks)]
    finals = [product(inverse[b], middles[b]) for b in range(blocks)]
    for b in range(blocks):
        flipped = finals[b].T
        inner = product(sides[b], flipped)
        shift = product(inner, flipped) / norms[b]
        out[b, :size] = flipped * (math.sqrt(size - 1.0) / jnp.sqrt(norms[b]))
        out[b, size:] = shift


def transforms(own, *halo):
    total, lines, size = own.shape
    blocks = len(halo) or total - 2
    return pl.pallas_call(
        partial(transform_kernel, bool(halo)),
        out_shape=jax.ShapeDtypeStruct((blocks, lines, size), F32),
        scratch_shapes=[
            pltpu.VMEM((blocks, size, size), F32),
            pltpu.VMEM((blocks, size, size), F32),
        ],
        name="transform",
        compiler_params=pltpu.CompilerParams(vmem_limit_bytes=16 << 20),
    )(own, *halo)


def apply_kernel(share, pieces, *refs):
    states, (inner, outer, out) = refs[:pieces], refs[pieces:]
    block = pl.program_id(0)
    within = (block > 0) & (block < pl.num_programs(0) - 1)
    cells = jnp.concatenate([piece[0] for piece in states], 0)
    members, width = cells.shape
    rows = width // LANES
    weights = jnp.where(within, inner[0], outer[0])
    centre = jnp.sum(cells, axis=0, keepdims=True) * (1.0 / members)
    moved = product(weights, cells - centre)
    common = centre + moved[members : members + 1]
    common_high, common_low = halves(
        jnp.concatenate([common[:, r * LANES : (r + 1) * LANES] for r in range(rows)], 0)
    )
    for part in range(members // share):
        for r in range(rows):
            out[0, part, r * share : (r + 1) * share] = moved[
                part * share : (part + 1) * share, r * LANES : (r + 1) * LANES
            ].astype(BF16)
        out[0, part, rows * share : rows * share + rows] = common_high
        out[0, part, rows * share + rows :] = common_low


def apply_transform(share, begin, rows, states, inner, outer):
    blocks = states[0].shape[0]
    members = sum(piece.shape[1] for piece in states)
    lines = rows * (share + 2)
    return pl.pallas_call(
        partial(apply_kernel, share, len(states)),
        grid=(blocks,),
        in_specs=[
            *[
                pl.BlockSpec((1, piece.shape[1], rows * LANES), lambda i: (i, 0, begin))
                for piece in states
            ],
            pl.BlockSpec(
                (1, members + 8, members), lambda i: (jnp.clip(i - 1, 0, blocks - 3), 0, 0)
            ),
            pl.BlockSpec((1, members + 8, members), lambda i: (i // (blocks - 1), 0, 0)),
        ],
        out_specs=pl.BlockSpec((1, members // share, lines, LANES), lambda i: (i, 0, 0, 0)),
        out_shape=jax.ShapeDtypeStruct((blocks, members // share, lines, LANES), BF16),
        name="apply",
        compiler_params=pltpu.CompilerParams(vmem_limit_bytes=20 << 20),
    )(*states, inner, outer)


def unpack_kernel(share, rows, *refs):
    *chunks, out, stage = refs
    for part in range(PLANE):
        cols = slice(part * LANES, (part + 1) * LANES)
        for half, chunk in enumerate(chunks):
            common = chunk[part, 0, rows * share :].astype(F32)
            common = common[:rows] + common[rows:]
            for r in range(rows):
                field = chunk[part, 0, r * share : (r + 1) * share].astype(F32) + common[r : r + 1]
                for k in range(share // 8):
                    stage[part, pl.ds(64 * k + half * rows + r, 8, stride=8)] = field[
                        8 * k : 8 * k + 8
                    ]
        out[:, cols] = stage[part]


def unpack(share, rows, chunks):
    _, groups, lines, _ = chunks[0].shape
    return pl.pallas_call(
        partial(unpack_kernel, share, rows),
        grid=(groups,),
        in_specs=[pl.BlockSpec((PLANE, 1, lines, LANES), lambda i: (0, i, 0, 0))] * len(chunks),
        out_specs=pl.BlockSpec((share * ROWS, PLANE * LANES), lambda i: (0, i)),
        out_shape=jax.ShapeDtypeStruct((share * ROWS, groups * PLANE * LANES), F32),
        scratch_shapes=[pltpu.VMEM((PLANE, share * ROWS, LANES), F32)],
        name="unpack",
        compiler_params=pltpu.CompilerParams(vmem_limit_bytes=12 << 20),
    )(*chunks)


def local(prior, drive, value, index, weight):
    members, rows, cols = prior.shape
    groups = lax.axis_size("member")
    planes = lax.axis_size("y")
    plane = lax.axis_index("y")
    upward = [(i + 1, i) for i in range(planes - 1)]
    downward = [(i, i + 1) for i in range(planes - 1)]
    me = jnp.stack([lax.axis_index("member"), lax.axis_index("zc")]).astype(jnp.int32)
    inside = jnp.stack([plane > 0, plane < planes - 1]).astype(F32)
    axes = ("zc", "member")
    tied = lax.optimization_barrier
    chunk, drive = tied((pack(prior), drive))
    outward = [
        (PLANE * i + edge, PLANE * j + edge)
        for edge, pairs in ((0, upward), (PLANE - 1, downward))
        for i, j in pairs
    ]
    extra = pack_extra(me, cols, drive, value, index, weight)
    outer_rows = lax.ppermute(extra, ("y", "zc"), outward)
    pieces = [jnp.concatenate([extra[d], outer_rows[d]], 0) for d in range(PLANE)]
    for d in range(1, PLANE):
        pieces[d] = lax.ppermute(
            pieces[d], "zc", [(i, (i + d) % PLANE) for i in range(PLANE)]
        )
    extra, force = forcing(me, pieces)
    chunk = lax.all_to_all(chunk, axes, 0, 0, tiled=True)
    cells = chunk.reshape(PLANE, groups, ROWS + 1, members, LANES)
    bottom = lax.ppermute(cells[0], "y", upward)
    top = lax.ppermute(cells[PLANE - 1], "y", downward)
    states = (forecast(inside, cells, top, bottom, force),)
    own, up, down = curvatures(states, extra)
    from_below = lax.ppermute(up, "y", upward)
    from_above = lax.ppermute(down, "y", downward)
    inner = transforms(own)
    outer = transforms(own, from_above, from_below)
    analysed = apply_transform(members, 0, ROWS, states, inner, outer)
    sent = analysed.reshape(PLANE * groups, *analysed.shape[2:])
    back = lax.all_to_all(sent, axes, 0, 0, tiled=True).reshape(analysed.shape)
    return unpack(members, ROWS, [back]).reshape(members, rows, cols)


def solution(mesh):
    groups, spaces = mesh.devices.shape
    fine = Mesh(mesh.devices.reshape(groups, spaces // PLANE, PLANE), ("member", "y", "zc"))
    rows = ("y", "zc")
    return jax.shard_map(
        local,
        mesh=fine,
        in_specs=(
            P("member", rows, None),
            P(rows, None),
            P(rows, "member", None),
            P(rows, "member", None),
            P(rows, "member", None),
        ),
        out_specs=P("member", rows, None),
        check_vma=False,
    )
```

```python
import math
from functools import partial

import jax
import jax.numpy as jnp
from jax import lax
from jax.experimental import pallas as pl
from jax.experimental.pallas import tpu as pltpu
from jax.sharding import Mesh, PartitionSpec as P


STEPS = 8
ITERS = 6
ROWS = 8
LANES = 128
PLANE = 4
F32 = jnp.float32
BF16 = jnp.bfloat16


def lane_index(rows):
    return lax.broadcasted_iota(jnp.int32, (rows, LANES), 1)


def halves(x):
    high = x.astype(BF16)
    return high, (x - high.astype(F32)).astype(BF16)


def thirds(x):
    high = x.astype(BF16)
    rest = x - high.astype(F32)
    mid = rest.astype(BF16)
    return high, mid, (rest - mid.astype(F32)).astype(BF16)


def product(a, b):
    ah, al = halves(a)
    bh, bl = halves(b)
    return jnp.dot(
        jnp.concatenate([ah, ah, al], 1),
        jnp.concatenate([bh, bl, bh], 0),
        preferred_element_type=F32,
    )


def against_rows(a, b):
    return lax.dot_general(a, b, (((1,), (1,)), ((), ())), preferred_element_type=F32)


def to_tile(line):
    return jnp.concatenate([line[:, r * LANES : (r + 1) * LANES] for r in range(ROWS)], 0)


def to_line(tile):
    return jnp.concatenate([tile[r : r + 1] for r in range(ROWS)], 1)


def pack_kernel(tiles, prior, chunk, stage):
    lane = lane_index(16)
    groups = tiles // PLANE

    def place(tile):
        return lax.rem(tile, PLANE) * groups + tile // PLANE

    def rounding(tile, carry):
        cols = pl.ds(pl.multiple_of(tile * LANES, LANES), LANES)
        left = [jnp.zeros((16, LANES), F32)] * 2
        slot = lax.rem(tile, 4)
        stage[slot] = prior[:, cols]
        for row in range(ROWS):
            cells = jnp.concatenate(
                [stage[slot, pl.ds(row, 8, stride=8)], stage[slot, pl.ds(64 + row, 8, stride=8)]], 0
            )
            wanted = cells + left[row % 2]
            kept = wanted.astype(BF16)
            left[row % 2] = wanted - kept.astype(F32)
            chunk[place(tile), row] = kept
        return carry

    lax.fori_loop(0, tiles, rounding, 0, unroll=4)

    def edges(tile, carry):
        before = place(lax.rem(tile + tiles - 1, tiles))
        after = place(lax.rem(tile + 1, tiles))
        total = jnp.zeros((16, LANES), F32)
        for row in range(ROWS):
            both = jnp.where(
                lane >= LANES // 2, chunk[before, row].astype(F32), chunk[after, row].astype(F32)
            )
            moved = pltpu.roll(both, (16 * row + 8) % LANES, 1)
            total = jnp.where(lane // 16 == row, moved, total)
        chunk[place(tile), ROWS] = total.astype(BF16)
        return carry

    lax.fori_loop(0, tiles, edges, 0, unroll=4)


def extra_kernel(tiles, me_ref, drive, value, index, weight, extra):
    lane8 = lane_index(8)
    weights = weight[0].astype(F32)
    slot4 = lax.broadcasted_iota(jnp.int32, weights.shape, 0)
    for ahead in range(PLANE):
        part = lax.rem(me_ref[1] + ahead, PLANE)
        tile = me_ref[0] * PLANE + part

        def forcing(t):
            return drive[:, pl.ds(pl.multiple_of(lax.rem(t + tiles, tiles) * LANES, LANES), LANES)]

        main = forcing(tile)
        both = jnp.where(lane8 >= LANES // 2, forcing(tile - 1), forcing(tile + 1))
        chosen = slot4 == part
        for slot, field in ((0, value[0]), (1, index[0].astype(F32)), (2, weights)):
            line = jnp.sum(jnp.where(chosen, field, 0.0), axis=0, keepdims=True)
            extra[ahead, slot : slot + 1, :] = line
        extra[ahead, 5:8, :] = jnp.zeros((3, ROWS * LANES), F32)
        for slot, field in ((3, main), (4, both)):
            for row in range(ROWS):
                extra[ahead, slot : slot + 1, row * LANES : (row + 1) * LANES] = field[row : row + 1]


def pack_extra(me, cols, drive, value, index, weight):
    return pl.pallas_call(
        partial(extra_kernel, cols // LANES),
        in_specs=[pl.BlockSpec(memory_space=pltpu.SMEM)]
        + [pl.BlockSpec(memory_space=pltpu.VMEM)] * 4,
        out_shape=jax.ShapeDtypeStruct((PLANE, 8, ROWS * LANES), F32),
        name="pack_extra",
        compiler_params=pltpu.CompilerParams(vmem_limit_bytes=8 << 20),
    )(me, drive, value, index, weight)


def pack(prior):
    members, rows, cols = prior.shape
    tiles = cols // LANES
    part = members // 2
    return pl.pallas_call(
        partial(pack_kernel, tiles),
        grid=(2,),
        in_specs=[pl.BlockSpec((part * rows, cols), lambda i: (i, 0))],
        out_specs=pl.BlockSpec((tiles, ROWS + 1, part, LANES), lambda i: (0, 0, i, 0)),
        out_shape=jax.ShapeDtypeStruct((tiles, ROWS + 1, members, LANES), BF16),
        scratch_shapes=[pltpu.VMEM((4, part * rows, LANES), F32)],
        name="pack",
    )(prior.reshape(members * rows, cols))


def force_kernel(me_ref, own, one, two, three, extra, force, halo):
    for behind, came in enumerate((own, one, two, three)):
        strip = lax.rem(me_ref[1] + PLANE - behind, PLANE)
        extra[strip] = came[:8]
        halo[strip] = came[8:]
    lane = lane_index(8)
    for strip in range(PLANE + 2):
        if strip == 0:
            source = halo.at[PLANE - 1]
        elif strip == PLANE + 1:
            source = halo.at[0]
        else:
            source = extra.at[strip - 1]
        main = to_tile(source[3:4]) * 0.005
        both = to_tile(source[4:5]) * 0.005
        for b in range(8):
            line = pltpu.roll(main, (LANES + 8 - 32 * (b % 4)) % LANES, 1)
            if b % 4 == 0:
                line = jnp.where(lane < 8, pltpu.roll(both, 8, 1), line)
            if b % 4 == 3:
                line = jnp.where(lane >= 40, pltpu.roll(both, 40, 1), line)
            force[pl.ds(strip * 8 * ROWS + b, 8, stride=8)] = line


def forcing(me, pieces):
    width = pieces[0].shape[1]
    return pl.pallas_call(
        force_kernel,
        in_specs=[pl.BlockSpec(memory_space=pltpu.SMEM)]
        + [pl.BlockSpec(memory_space=pltpu.VMEM)] * PLANE,
        out_shape=[
            jax.ShapeDtypeStruct((PLANE, 8, width), F32),
            jax.ShapeDtypeStruct(((PLANE + 2) * ROWS * 8, LANES), F32),
        ],
        scratch_shapes=[pltpu.VMEM((PLANE, 8, width), F32)],
        name="forcing",
        compiler_params=pltpu.CompilerParams(vmem_limit_bytes=8 << 20),
    )(me, *pieces)


def load_strip(source, strip, force, now, push, turned):
    span = now.shape[1]
    lane = lane_index(LANES)
    unit = jnp.where(lax.broadcasted_iota(jnp.int32, lane.shape, 0) == lane, 1.0, 0.0).astype(BF16)
    line = lax.broadcasted_iota(jnp.int32, (8 * span, 2 * LANES), 0)
    sub = lax.rem(line, 8)
    wanted = 32 * lax.rem(sub, 4) + line // 8 - 8
    place = lax.broadcasted_iota(jnp.int32, line.shape, 1)
    spread = (lax.rem(place, LANES) == wanted) & (place // LANES == sub // 4)
    spread = jnp.where(spread, 1.0, 0.0).astype(BF16)
    for h in range(2):
        edge = source[4 * h : 4 * h + 4, ROWS].reshape(LANES, LANES)
        turned[0, h * LANES : (h + 1) * LANES] = against_rows(unit, edge) * 0.05

    def load(i, carry):
        for k in range(4):
            r = 4 * i + k
            row = strip * ROWS + r
            both = jnp.concatenate(
                [source[4 * h : 4 * h + 4, r].reshape(LANES, LANES) for h in range(2)], 1
            )
            main = against_rows(spread, both) * 0.05
            for c in range(span):
                now[row, c] = main[8 * c : 8 * c + 8]
            at = pl.multiple_of(16 * r, 16)
            for h in range(2):
                for c in range(8):
                    low = turned[0, pl.ds(h * LANES + at + c, 1)]
                    high = turned[0, pl.ds(h * LANES + at + 8 + c, 1)]
                    now[row, c, 4 * h : 4 * h + 1] = low
                    now[row, span - 8 + c, 4 * h + 3 : 4 * h + 4] = high
            pushes = force[pl.ds(pl.multiple_of(row * 8, 8), 8)]
            for c in range(span):
                push[row, c] = jnp.broadcast_to(pushes[:, c : c + 1], (8, LANES))
        return carry

    lax.fori_loop(0, ROWS // 4, load, 0)


def advance(step, first, last, source, target, push):
    low, high = step + 1, source.shape[1] - 2 - step

    def pair(i, carry):
        row = first + 2 * i
        west = [source[row + k, low - 1] for k in range(2)]
        here = [source[row + k, low] for k in range(2)]
        for c in range(low, high + 1):
            east = [source[row + k, c + 1] for k in range(2)]
            column = [source[row - 1, c], *here, source[row + 2, c]]
            for k in range(2):
                above, below = column[k], column[k + 2]
                turn = (west[k] - east[k]) + (above - below) + 0.05
                target[row + k, c] = (
                    push[row + k, c]
                    + here[k] * turn
                    + 0.05 * (east[k] + west[k])
                    + 0.4 * (above + below)
                )
            west, here = here, east
        return carry

    lax.fori_loop(0, (last + 1 - first) // 2, pair, 0)


def inner_kernel(cells, force, now, later, push, turned):
    for strip in range(PLANE):
        load_strip(cells.at[strip], strip + 1, force, now, push, turned)
    depth = now.shape[0]
    fields = (now, later)
    for step in range(STEPS):
        first = ROWS + 1 + step
        advance(step, first, depth - 1 - first, fields[step % 2], fields[1 - step % 2], push)


def outer_kernel(inside, top, bottom, force, *refs):
    out, now, later, push, turned = refs[3:]
    depth, span = now.shape[:2]
    load_strip(top, 0, force, now, push, turned)
    load_strip(bottom, PLANE + 1, force, now, push, turned)
    keep_top, keep_bottom = inside[0], inside[1]
    fields = (now, later)
    for step in range(STEPS):
        source, target = fields[step % 2], fields[1 - step % 2]
        first, last = step + 1, ROWS + step
        advance(step, first, last, source, target, push)
        advance(step, depth - 1 - last, depth - 1 - first, source, target, push)
        if step < STEPS - 1:
            for c in range(step + 1, span - 1 - step):
                target[ROWS - 1, c] = target[ROWS - 1, c] * keep_top
                target[depth - ROWS, c] = target[depth - ROWS, c] * keep_bottom
    source = fields[STEPS % 2]
    for strip in range(PLANE):

        def save(i, carry):
            for k in range(2):
                row = (strip + 1) * ROWS + 2 * i + k
                for c in range(span - 16):
                    turned[k, 8 * c : 8 * c + 8] = 20.0 * source[row, c + 8]
            for k in range(2):
                at = pl.multiple_of((2 * i + k) * LANES, LANES)
                for h in range(2):
                    columns = [
                        turned[k, pl.ds(64 * c + 4 * h + b, 8, stride=8)]
                        for b in range(4)
                        for c in range(4)
                    ]
                    part = slice(h * LANES, (h + 1) * LANES)
                    out[strip, part, pl.ds(at, LANES)] = jnp.concatenate(columns, 0).T
            return carry

        lax.fori_loop(0, ROWS // 2, save, 0)


def forecast_inner(cells, force):
    field = ((PLANE + 2) * ROWS, 48, 8, LANES)
    vmem = pl.BlockSpec(memory_space=pltpu.VMEM)
    return pl.pallas_call(
        inner_kernel,
        in_specs=[vmem, vmem],
        out_specs=[vmem] * 3,
        out_shape=[jax.ShapeDtypeStruct(field, F32)] * 3,
        scratch_shapes=[pltpu.VMEM((1, 2 * LANES, LANES), F32)],
        name="forecast_inner",
        compiler_params=pltpu.CompilerParams(vmem_limit_bytes=4 << 20),
    )(cells, force)


def forecast_outer(inside, top, bottom, force, *fields):
    vmem = pl.BlockSpec(memory_space=pltpu.VMEM)
    return pl.pallas_call(
        outer_kernel,
        in_specs=[pl.BlockSpec(memory_space=pltpu.SMEM)] + [vmem] * 6,
        out_specs=[vmem] * 4,
        out_shape=[jax.ShapeDtypeStruct((PLANE, 2 * LANES, ROWS * LANES), F32)]
        + [jax.ShapeDtypeStruct(field.shape, F32) for field in fields],
        input_output_aliases={4: 1, 5: 2, 6: 3},
        scratch_shapes=[pltpu.VMEM((2, 2 * LANES, LANES), F32)],
        name="forecast_outer",
        compiler_params=pltpu.CompilerParams(vmem_limit_bytes=4 << 20),
    )(inside, top, bottom, force, *fields)[0]


def curvature_kernel(pieces, *refs):
    states, (obs, own, up, down) = refs[:pieces], refs[pieces:]
    block = pl.program_id(0)
    blocks = pl.num_programs(0)
    cells = jnp.concatenate([piece[0] for piece in states], 0)
    members = cells.shape[0]
    centre = jnp.sum(cells, axis=0, keepdims=True) * (1.0 / members)
    anomaly = (cells - centre).astype(BF16)
    value, index, weight = obs[0, 0:1], obs[0, 1:2], obs[0, 2:3]
    row_of = jnp.floor(index * (1.0 / LANES))
    col_of = index - row_of * LANES
    count = index.shape[1]
    in_row = lax.broadcasted_iota(jnp.int32, (ROWS, count), 0).astype(F32) == row_of
    in_col = jnp.where(
        lax.broadcasted_iota(jnp.int32, (LANES, count), 0).astype(F32) == col_of, 1.0, 0.0
    ).astype(BF16)
    parts = jnp.concatenate(thirds(to_tile(centre)), 0)
    seen = jnp.dot(parts, in_col, preferred_element_type=F32)
    seen = (seen[:ROWS] + seen[ROWS : 2 * ROWS]) + seen[2 * ROWS :]
    obs_mean = jnp.sum(jnp.where(in_row, seen, 0.0), axis=0, keepdims=True)
    innovation = (value - obs_mean).astype(BF16).astype(F32)
    pull_high, pull_low = halves(weight * innovation)
    spread = jnp.concatenate(
        [
            jnp.where(in_row, weight, 0.0),
            jnp.where(in_row, pull_high.astype(F32), 0.0),
            jnp.where(in_row, pull_low.astype(F32), 0.0),
        ],
        0,
    ).astype(BF16)
    summed = against_rows(spread, in_col)
    weights = summed[:ROWS]
    pulls = summed[ROWS : 2 * ROWS] + summed[2 * ROWS :]
    row_pos = lax.broadcasted_iota(jnp.int32, (ROWS, LANES), 0).astype(F32)
    span = float(ROWS)
    fall_down = jnp.exp(-2.0 * (span - row_pos) * (span - row_pos) / (span * span))
    fall_up = jnp.exp(-2.0 * (row_pos + 1.0) * (row_pos + 1.0) / (span * span))
    wide = anomaly.astype(F32)
    ones = jnp.ones((ROWS, LANES), F32)
    factors = (ones, fall_up, fall_down)
    terms = [
        against_rows((wide * to_line(weights * f)).astype(BF16), anomaly) for f in factors
    ]
    lines = []
    for f in factors:
        lines.extend(thirds(to_line(pulls * f)))
    lines.append(jnp.zeros((7, count), BF16))
    vectors = against_rows(jnp.concatenate(lines, 0), anomaly)
    sides = [
        (vectors[3 * i : 3 * i + 1] + vectors[3 * i + 1 : 3 * i + 2]) + vectors[3 * i + 2 : 3 * i + 3]
        for i in range(3)
    ]
    pad = jnp.zeros((7, members), F32)

    @pl.when(block == 0)
    def _():
        own[...] = jnp.zeros_like(own)
        up[:members] = terms[1]
        up[members:] = jnp.concatenate([sides[1], pad], 0)

    own[block, :members] += terms[0]
    own[block, members:] += jnp.concatenate([sides[0], pad], 0)

    @pl.when(block > 0)
    def _():
        own[block - 1, :members] += terms[1]
        own[block - 1, members:] += jnp.concatenate([sides[1], pad], 0)

    @pl.when(block < blocks - 1)
    def _():
        own[block + 1, :members] += terms[2]
        own[block + 1, members:] += jnp.concatenate([sides[2], pad], 0)

    @pl.when(block == blocks - 1)
    def _():
        down[:members] = terms[2]
        down[members:] = jnp.concatenate([sides[2], pad], 0)


def of_block(states):
    return [pl.BlockSpec((1, *piece.shape[1:]), lambda i: (i, 0, 0)) for piece in states]


def curvatures(states, obs):
    blocks, _, width = states[0].shape
    members = sum(piece.shape[1] for piece in states)
    whole = lambda shape: pl.BlockSpec(shape, lambda i: (0,) * len(shape))
    return pl.pallas_call(
        partial(curvature_kernel, len(states)),
        grid=(blocks,),
        in_specs=[*of_block(states), pl.BlockSpec((1, 8, width), lambda i: (i, 0, 0))],
        out_specs=[
            whole((blocks, members + 8, members)),
            whole((members + 8, members)),
            whole((members + 8, members)),
        ],
        out_shape=[
            jax.ShapeDtypeStruct((blocks, members + 8, members), F32),
            jax.ShapeDtypeStruct((members + 8, members), F32),
            jax.ShapeDtypeStruct((members + 8, members), F32),
        ],
        name="curvature",
        compiler_params=pltpu.CompilerParams(vmem_limit_bytes=16 << 20),
    )(*states, obs)


def transform_kernel(edges, *refs):
    own, *rest = refs
    *halo, out, iterate, inverse = rest
    blocks, size, _ = iterate.shape
    row = lax.broadcasted_iota(jnp.int32, (size, size), 0)
    col = lax.broadcasted_iota(jnp.int32, (size, size), 1)
    diagonal = row == col

    def middle_of(x):
        return jnp.where(diagonal, 1.5 - 0.5 * x, -0.5 * x)

    norms, sides = [], []
    for b in range(blocks):
        place = b * (own.shape[0] - 1) if edges else b + 1
        matrix, side = own[place, :size], own[place, size:]
        if edges:
            matrix, side = matrix + halo[b][:size], side + halo[b][size:]
        matrix = matrix + jnp.where(diagonal, size - 1.0, 0.0)
        squares = jnp.sum(jnp.sum(matrix * matrix, axis=0, keepdims=True), axis=1, keepdims=True)
        norm = jnp.sqrt(squares)
        start = matrix / norm
        middle = middle_of(start)
        inverse[b] = middle
        iterate[b] = product(start, middle)
        norms.append(norm)
        sides.append(side)

    def sweep(i, carry):
        middles = [middle_of(product(inverse[b], iterate[b])) for b in range(blocks)]
        for b in range(blocks):
            both = product(jnp.concatenate([iterate[b], inverse[b]], 0), middles[b])
            iterate[b] = both[:size]
            inverse[b] = both[size:]
        return carry

    lax.fori_loop(0, ITERS - 2, sweep, 0)
    middles = [middle_of(product(inverse[b], iterate[b])) for b in range(blocks)]
    finals = [product(inverse[b], middles[b]) for b in range(blocks)]
    for b in range(blocks):
        flipped = finals[b].T
        inner = product(sides[b], flipped)
        shift = product(inner, flipped) / norms[b]
        out[b, :size] = flipped * (math.sqrt(size - 1.0) / jnp.sqrt(norms[b]))
        out[b, size:] = shift


def transforms(own, *halo):
    total, lines, size = own.shape
    blocks = len(halo) or total - 2
    return pl.pallas_call(
        partial(transform_kernel, bool(halo)),
        out_shape=jax.ShapeDtypeStruct((blocks, lines, size), F32),
        scratch_shapes=[
            pltpu.VMEM((blocks, size, size), F32),
            pltpu.VMEM((blocks, size, size), F32),
        ],
        name="transform",
        compiler_params=pltpu.CompilerParams(vmem_limit_bytes=16 << 20),
    )(own, *halo)


def apply_kernel(share, pieces, *refs):
    states, (inner, outer, out) = refs[:pieces], refs[pieces:]
    block = pl.program_id(0)
    within = (block > 0) & (block < pl.num_programs(0) - 1)
    cells = jnp.concatenate([piece[0] for piece in states], 0)
    members, width = cells.shape
    rows = width // LANES
    weights = jnp.where(within, inner[0], outer[0])
    centre = jnp.sum(cells, axis=0, keepdims=True) * (1.0 / members)
    moved = product(weights, cells - centre)
    common = centre + moved[members : members + 1]
    common_high, common_low = halves(
        jnp.concatenate([common[:, r * LANES : (r + 1) * LANES] for r in range(rows)], 0)
    )
    for part in range(members // share):
        for r in range(rows):
            out[0, part, r * share : (r + 1) * share] = moved[
                part * share : (part + 1) * share, r * LANES : (r + 1) * LANES
            ].astype(BF16)
        out[0, part, rows * share : rows * share + rows] = common_high
        out[0, part, rows * share + rows :] = common_low


def apply_transform(share, begin, rows, states, inner, outer):
    blocks = states[0].shape[0]
    members = sum(piece.shape[1] for piece in states)
    lines = rows * (share + 2)
    return pl.pallas_call(
        partial(apply_kernel, share, len(states)),
        grid=(blocks,),
        in_specs=[
            *[
                pl.BlockSpec((1, piece.shape[1], rows * LANES), lambda i: (i, 0, begin))
                for piece in states
            ],
            pl.BlockSpec(
                (1, members + 8, members), lambda i: (jnp.clip(i - 1, 0, blocks - 3), 0, 0)
            ),
            pl.BlockSpec((1, members + 8, members), lambda i: (i // (blocks - 1), 0, 0)),
        ],
        out_specs=pl.BlockSpec((1, members // share, lines, LANES), lambda i: (i, 0, 0, 0)),
        out_shape=jax.ShapeDtypeStruct((blocks, members // share, lines, LANES), BF16),
        name="apply",
        compiler_params=pltpu.CompilerParams(vmem_limit_bytes=20 << 20),
    )(*states, inner, outer)


def unpack_kernel(share, rows, *refs):
    *chunks, out, stage = refs
    for part in range(PLANE):
        cols = slice(part * LANES, (part + 1) * LANES)
        for half, chunk in enumerate(chunks):
            common = chunk[part, 0, rows * share :].astype(F32)
            common = common[:rows] + common[rows:]
            for r in range(rows):
                field = chunk[part, 0, r * share : (r + 1) * share].astype(F32) + common[r : r + 1]
                for k in range(share // 8):
                    stage[part, pl.ds(64 * k + half * rows + r, 8, stride=8)] = field[
                        8 * k : 8 * k + 8
                    ]
        out[:, cols] = stage[part]


def unpack(share, rows, chunks):
    _, groups, lines, _ = chunks[0].shape
    return pl.pallas_call(
        partial(unpack_kernel, share, rows),
        grid=(groups,),
        in_specs=[pl.BlockSpec((PLANE, 1, lines, LANES), lambda i: (0, i, 0, 0))] * len(chunks),
        out_specs=pl.BlockSpec((share * ROWS, PLANE * LANES), lambda i: (0, i)),
        out_shape=jax.ShapeDtypeStruct((share * ROWS, groups * PLANE * LANES), F32),
        scratch_shapes=[pltpu.VMEM((PLANE, share * ROWS, LANES), F32)],
        name="unpack",
        compiler_params=pltpu.CompilerParams(vmem_limit_bytes=12 << 20),
    )(*chunks)


def local(prior, drive, value, index, weight):
    members, rows, cols = prior.shape
    groups = lax.axis_size("member")
    planes = lax.axis_size("y")
    plane = lax.axis_index("y")
    upward = [(i + 1, i) for i in range(planes - 1)]
    downward = [(i, i + 1) for i in range(planes - 1)]
    me = jnp.stack([lax.axis_index("member"), lax.axis_index("zc")]).astype(jnp.int32)
    inside = jnp.stack([plane > 0, plane < planes - 1]).astype(F32)
    axes = ("zc", "member")
    tied = lax.optimization_barrier
    chunk, drive = tied((pack(prior), drive))
    outward = [
        (PLANE * i + edge, PLANE * j + edge)
        for edge, pairs in ((0, upward), (PLANE - 1, downward))
        for i, j in pairs
    ]
    extra = pack_extra(me, cols, drive, value, index, weight)
    outer_rows = lax.ppermute(extra, ("y", "zc"), outward)
    pieces = [jnp.concatenate([extra[d], outer_rows[d]], 0) for d in range(PLANE)]
    for d in range(1, PLANE):
        pieces[d] = lax.ppermute(
            pieces[d], "zc", [(i, (i + d) % PLANE) for i in range(PLANE)]
        )
    extra, force = forcing(me, pieces)
    chunk = lax.all_to_all(chunk, axes, 0, 0, tiled=True)
    cells = chunk.reshape(PLANE, groups, ROWS + 1, members, LANES)
    bottom = lax.ppermute(cells[0], "y", upward)
    top = lax.ppermute(cells[PLANE - 1], "y", downward)
    fields = forecast_inner(cells, force)
    states = (forecast_outer(inside, top, bottom, force, *fields),)
    own, up, down = curvatures(states, extra)
    from_below = lax.ppermute(up, "y", upward)
    from_above = lax.ppermute(down, "y", downward)
    inner = transforms(own)
    outer = transforms(own, from_above, from_below)
    analysed = apply_transform(members, 0, ROWS, states, inner, outer)
    sent = analysed.reshape(PLANE * groups, *analysed.shape[2:])
    back = lax.all_to_all(sent, axes, 0, 0, tiled=True).reshape(analysed.shape)
    return unpack(members, ROWS, [back]).reshape(members, rows, cols)


def solution(mesh):
    groups, spaces = mesh.devices.shape
    fine = Mesh(mesh.devices.reshape(groups, spaces // PLANE, PLANE), ("member", "y", "zc"))
    rows = ("y", "zc")
    return jax.shard_map(
        local,
        mesh=fine,
        in_specs=(
            P("member", rows, None),
            P(rows, None),
            P(rows, "member", None),
            P(rows, "member", None),
            P(rows, "member", None),
        ),
        out_specs=P("member", rows, None),
        check_vma=False,
    )
```

```python
import math
from functools import partial

import jax
import jax.numpy as jnp
from jax import lax
from jax.experimental import pallas as pl
from jax.experimental.pallas import tpu as pltpu
from jax.sharding import Mesh, PartitionSpec as P


STEPS = 8
ITERS = 6
ROWS = 8
LANES = 128
PLANE = 4
F32 = jnp.float32
BF16 = jnp.bfloat16


def lane_index(rows):
    return lax.broadcasted_iota(jnp.int32, (rows, LANES), 1)


def halves(x):
    high = x.astype(BF16)
    return high, (x - high.astype(F32)).astype(BF16)


def thirds(x):
    high = x.astype(BF16)
    rest = x - high.astype(F32)
    mid = rest.astype(BF16)
    return high, mid, (rest - mid.astype(F32)).astype(BF16)


def product(a, b):
    ah, al = halves(a)
    bh, bl = halves(b)
    return jnp.dot(
        jnp.concatenate([ah, ah, al], 1),
        jnp.concatenate([bh, bl, bh], 0),
        preferred_element_type=F32,
    )


def against_rows(a, b):
    return lax.dot_general(a, b, (((1,), (1,)), ((), ())), preferred_element_type=F32)


def to_tile(line):
    return jnp.concatenate([line[:, r * LANES : (r + 1) * LANES] for r in range(ROWS)], 0)


def to_line(tile):
    return jnp.concatenate([tile[r : r + 1] for r in range(ROWS)], 1)


def pack_kernel(main, before, after, chunk, stage, kept):
    share = main.shape[0] // ROWS
    count = main.shape[1] // LANES
    lane = lane_index(share)

    def rounding(field, cols, place, slot):
        stage[slot] = field[:, cols]
        left = [jnp.zeros((share, LANES), F32)] * 2
        for row in range(ROWS):
            wanted = left[row % 2] + jnp.concatenate(
                [stage[slot, pl.ds(8 * ROWS * k + row, 8, stride=ROWS)] for k in range(share // 8)], 0
            )
            cells = wanted.astype(BF16)
            value = cells.astype(F32)
            left[row % 2] = wanted - value
            kept[place, row] = value
            if not isinstance(place, int):
                chunk[lax.rem(place - 1, PLANE), (place - 1) // PLANE, row] = cells

    def tile(t, carry):
        cols = pl.ds(pl.multiple_of(t * LANES, LANES), LANES)
        rounding(main, cols, t + 1, lax.rem(t, 4))
        return carry

    rounding(before, slice(0, LANES), 0, 0)
    rounding(after, slice(0, LANES), count + 1, 1)
    lax.fori_loop(0, count, tile, 0, unroll=4)

    def edges(t, carry):
        total = jnp.zeros((share, LANES), F32)
        for row in range(ROWS):
            both = jnp.where(lane >= LANES // 2, kept[t, row], kept[t + 2, row])
            moved = pltpu.roll(both, (16 * row + 8) % LANES, 1)
            total = jnp.where(lane // 16 == row, moved, total)
        chunk[lax.rem(t, PLANE), t // PLANE, ROWS] = total.astype(BF16)
        return carry

    lax.fori_loop(0, count, edges, 0, unroll=4)


def extra_kernel(tiles, me_ref, drive, value, index, weight, extra):
    lane8 = lane_index(8)
    weights = weight[0].astype(F32)
    slot4 = lax.broadcasted_iota(jnp.int32, weights.shape, 0)
    for ahead in range(PLANE):
        part = lax.rem(me_ref[1] + ahead, PLANE)
        tile = me_ref[0] * PLANE + part

        def forcing(t):
            return drive[:, pl.ds(pl.multiple_of(lax.rem(t + tiles, tiles) * LANES, LANES), LANES)]

        main = forcing(tile)
        both = jnp.where(lane8 >= LANES // 2, forcing(tile - 1), forcing(tile + 1))
        chosen = slot4 == part
        for slot, field in ((0, value[0]), (1, index[0].astype(F32)), (2, weights)):
            line = jnp.sum(jnp.where(chosen, field, 0.0), axis=0, keepdims=True)
            extra[ahead, slot : slot + 1, :] = line
        extra[ahead, 5:8, :] = jnp.zeros((3, ROWS * LANES), F32)
        for slot, field in ((3, main), (4, both)):
            for row in range(ROWS):
                extra[ahead, slot : slot + 1, row * LANES : (row + 1) * LANES] = field[row : row + 1]


def pack_extra(me, cols, drive, value, index, weight):
    return pl.pallas_call(
        partial(extra_kernel, cols // LANES),
        in_specs=[pl.BlockSpec(memory_space=pltpu.SMEM)]
        + [pl.BlockSpec(memory_space=pltpu.VMEM)] * 4,
        out_shape=jax.ShapeDtypeStruct((PLANE, 8, ROWS * LANES), F32),
        name="pack_extra",
        compiler_params=pltpu.CompilerParams(vmem_limit_bytes=8 << 20),
    )(me, drive, value, index, weight)


def pack(prior):
    members, rows, cols = prior.shape
    tiles = cols // LANES
    steps = 4
    count = tiles // steps
    side = lambda step: pl.BlockSpec(
        (members * rows, LANES), lambda i: (0, lax.rem(count * i + step + tiles, tiles))
    )
    flat = prior.reshape(members * rows, cols)
    return pl.pallas_call(
        pack_kernel,
        grid=(steps,),
        in_specs=[
            pl.BlockSpec((members * rows, count * LANES), lambda i: (0, i)),
            side(-1),
            side(count),
        ],
        out_specs=pl.BlockSpec(
            (PLANE, count // PLANE, ROWS + 1, members, LANES), lambda i: (0, i, 0, 0, 0)
        ),
        out_shape=jax.ShapeDtypeStruct((PLANE, tiles // PLANE, ROWS + 1, members, LANES), BF16),
        scratch_shapes=[
            pltpu.VMEM((4, members * rows, LANES), F32),
            pltpu.VMEM((count + 2, ROWS, members, LANES), F32),
        ],
        name="pack",
    )(flat, flat, flat).reshape(tiles, ROWS + 1, members, LANES)


def force_kernel(me_ref, own, one, two, three, extra, force, halo):
    for behind, came in enumerate((own, one, two, three)):
        strip = lax.rem(me_ref[1] + PLANE - behind, PLANE)
        extra[strip] = came[:8]
        halo[strip] = came[8:]
    lane = lane_index(8)
    for strip in range(PLANE + 2):
        if strip == 0:
            source = halo.at[PLANE - 1]
        elif strip == PLANE + 1:
            source = halo.at[0]
        else:
            source = extra.at[strip - 1]
        main = to_tile(source[3:4]) * 0.005
        both = to_tile(source[4:5]) * 0.005
        for b in range(8):
            line = pltpu.roll(main, (LANES + 8 - 32 * (b % 4)) % LANES, 1)
            if b % 4 == 0:
                line = jnp.where(lane < 8, pltpu.roll(both, 8, 1), line)
            if b % 4 == 3:
                line = jnp.where(lane >= 40, pltpu.roll(both, 40, 1), line)
            force[pl.ds(strip * 8 * ROWS + b, 8, stride=8)] = line


def forcing(me, pieces):
    width = pieces[0].shape[1]
    return pl.pallas_call(
        force_kernel,
        in_specs=[pl.BlockSpec(memory_space=pltpu.SMEM)]
        + [pl.BlockSpec(memory_space=pltpu.VMEM)] * PLANE,
        out_shape=[
            jax.ShapeDtypeStruct((PLANE, 8, width), F32),
            jax.ShapeDtypeStruct(((PLANE + 2) * ROWS * 8, LANES), F32),
        ],
        scratch_shapes=[pltpu.VMEM((PLANE, 8, width), F32)],
        name="forcing",
        compiler_params=pltpu.CompilerParams(vmem_limit_bytes=8 << 20),
    )(me, *pieces)


def load_strip(source, strip, force, now, push, turned):
    span = now.shape[1]
    lane = lane_index(LANES)
    unit = jnp.where(lax.broadcasted_iota(jnp.int32, lane.shape, 0) == lane, 1.0, 0.0).astype(BF16)
    line = lax.broadcasted_iota(jnp.int32, (8 * span, 2 * LANES), 0)
    sub = lax.rem(line, 8)
    wanted = 32 * lax.rem(sub, 4) + line // 8 - 8
    place = lax.broadcasted_iota(jnp.int32, line.shape, 1)
    spread = (lax.rem(place, LANES) == wanted) & (place // LANES == sub // 4)
    spread = jnp.where(spread, 1.0, 0.0).astype(BF16)
    for h in range(2):
        edge = source[4 * h : 4 * h + 4, ROWS].reshape(LANES, LANES)
        turned[0, h * LANES : (h + 1) * LANES] = against_rows(unit, edge) * 0.05

    def load(i, carry):
        for k in range(4):
            r = 4 * i + k
            row = strip * ROWS + r
            both = jnp.concatenate(
                [source[4 * h : 4 * h + 4, r].reshape(LANES, LANES) for h in range(2)], 1
            )
            main = against_rows(spread, both) * 0.05
            for c in range(span):
                now[row, c] = main[8 * c : 8 * c + 8]
            at = pl.multiple_of(16 * r, 16)
            for h in range(2):
                for c in range(8):
                    low = turned[0, pl.ds(h * LANES + at + c, 1)]
                    high = turned[0, pl.ds(h * LANES + at + 8 + c, 1)]
                    now[row, c, 4 * h : 4 * h + 1] = low
                    now[row, span - 8 + c, 4 * h + 3 : 4 * h + 4] = high
            pushes = force[pl.ds(pl.multiple_of(row * 8, 8), 8)]
            for c in range(span):
                push[row, c] = jnp.broadcast_to(pushes[:, c : c + 1], (8, LANES))
        return carry

    lax.fori_loop(0, ROWS // 4, load, 0)


def advance(step, first, last, source, target, push):
    low, high = step + 1, source.shape[1] - 2 - step

    def pair(i, carry):
        row = first + 2 * i
        west = [source[row + k, low - 1] for k in range(2)]
        here = [source[row + k, low] for k in range(2)]
        for c in range(low, high + 1):
            east = [source[row + k, c + 1] for k in range(2)]
            column = [source[row - 1, c], *here, source[row + 2, c]]
            for k in range(2):
                above, below = column[k], column[k + 2]
                turn = (west[k] - east[k]) + (above - below) + 0.05
                target[row + k, c] = (
                    push[row + k, c]
                    + here[k] * turn
                    + 0.05 * (east[k] + west[k])
                    + 0.4 * (above + below)
                )
            west, here = here, east
        return carry

    lax.fori_loop(0, (last + 1 - first) // 2, pair, 0)


def inner_kernel(cells, force, now, later, push, turned):
    for strip in range(PLANE):
        load_strip(cells.at[strip], strip + 1, force, now, push, turned)
    depth = now.shape[0]
    fields = (now, later)
    for step in range(STEPS):
        first = ROWS + 1 + step
        advance(step, first, depth - 1 - first, fields[step % 2], fields[1 - step % 2], push)


def outer_kernel(inside, top, bottom, force, *refs):
    out, now, later, push, turned = refs[3:]
    depth, span = now.shape[:2]
    load_strip(top, 0, force, now, push, turned)
    load_strip(bottom, PLANE + 1, force, now, push, turned)
    keep_top, keep_bottom = inside[0], inside[1]
    fields = (now, later)
    for step in range(STEPS):
        source, target = fields[step % 2], fields[1 - step % 2]
        first, last = step + 1, ROWS + step
        advance(step, first, last, source, target, push)
        advance(step, depth - 1 - last, depth - 1 - first, source, target, push)
        if step < STEPS - 1:
            for c in range(step + 1, span - 1 - step):
                target[ROWS - 1, c] = target[ROWS - 1, c] * keep_top
                target[depth - ROWS, c] = target[depth - ROWS, c] * keep_bottom
    source = fields[STEPS % 2]
    for strip in range(PLANE):

        def save(i, carry):
            for k in range(2):
                row = (strip + 1) * ROWS + 2 * i + k
                for c in range(span - 16):
                    turned[k, 8 * c : 8 * c + 8] = 20.0 * source[row, c + 8]
            for k in range(2):
                at = pl.multiple_of((2 * i + k) * LANES, LANES)
                for h in range(2):
                    columns = [
                        turned[k, pl.ds(64 * c + 4 * h + b, 8, stride=8)]
                        for b in range(4)
                        for c in range(4)
                    ]
                    part = slice(h * LANES, (h + 1) * LANES)
                    out[strip, part, pl.ds(at, LANES)] = jnp.concatenate(columns, 0).T
            return carry

        lax.fori_loop(0, ROWS // 2, save, 0)


def forecast_inner(cells, force):
    field = ((PLANE + 2) * ROWS, 48, 8, LANES)
    vmem = pl.BlockSpec(memory_space=pltpu.VMEM)
    return pl.pallas_call(
        inner_kernel,
        in_specs=[vmem, vmem],
        out_specs=[vmem] * 3,
        out_shape=[jax.ShapeDtypeStruct(field, F32)] * 3,
        scratch_shapes=[pltpu.VMEM((1, 2 * LANES, LANES), F32)],
        name="forecast_inner",
        compiler_params=pltpu.CompilerParams(vmem_limit_bytes=4 << 20),
    )(cells, force)


def forecast_outer(inside, top, bottom, force, *fields):
    vmem = pl.BlockSpec(memory_space=pltpu.VMEM)
    return pl.pallas_call(
        outer_kernel,
        in_specs=[pl.BlockSpec(memory_space=pltpu.SMEM)] + [vmem] * 6,
        out_specs=[vmem] * 4,
        out_shape=[jax.ShapeDtypeStruct((PLANE, 2 * LANES, ROWS * LANES), F32)]
        + [jax.ShapeDtypeStruct(field.shape, F32) for field in fields],
        input_output_aliases={4: 1, 5: 2, 6: 3},
        scratch_shapes=[pltpu.VMEM((2, 2 * LANES, LANES), F32)],
        name="forecast_outer",
        compiler_params=pltpu.CompilerParams(vmem_limit_bytes=4 << 20),
    )(inside, top, bottom, force, *fields)[0]


def by_cell(states, obs):
    cells = states[0]
    members = cells.shape[0]
    centre = jnp.sum(cells, axis=0, keepdims=True) * (1.0 / members)
    anomaly = (cells - centre).astype(BF16)
    value, index, weight = obs[0, 0:1], obs[0, 1:2], obs[0, 2:3]
    row_of = jnp.floor(index * (1.0 / LANES))
    col_of = index - row_of * LANES
    count = index.shape[1]
    in_row = lax.broadcasted_iota(jnp.int32, (ROWS, count), 0).astype(F32) == row_of
    in_col = jnp.where(
        lax.broadcasted_iota(jnp.int32, (LANES, count), 0).astype(F32) == col_of, 1.0, 0.0
    ).astype(BF16)
    parts = jnp.concatenate(thirds(to_tile(centre)), 0)
    seen = jnp.dot(parts, in_col, preferred_element_type=F32)
    seen = (seen[:ROWS] + seen[ROWS : 2 * ROWS]) + seen[2 * ROWS :]
    obs_mean = jnp.sum(jnp.where(in_row, seen, 0.0), axis=0, keepdims=True)
    innovation = (value - obs_mean).astype(BF16).astype(F32)
    pull_high, pull_low = halves(weight * innovation)
    spread = jnp.concatenate(
        [
            jnp.where(in_row, weight, 0.0),
            jnp.where(in_row, pull_high.astype(F32), 0.0),
            jnp.where(in_row, pull_low.astype(F32), 0.0),
        ],
        0,
    ).astype(BF16)
    summed = against_rows(spread, in_col)
    weights = summed[:ROWS]
    pulls = summed[ROWS : 2 * ROWS] + summed[2 * ROWS :]
    return anomaly, weights, pulls


def falls():
    row_pos = lax.broadcasted_iota(jnp.int32, (ROWS, LANES), 0).astype(F32)
    span = float(ROWS)
    fall_down = jnp.exp(-2.0 * (span - row_pos) * (span - row_pos) / (span * span))
    fall_up = jnp.exp(-2.0 * (row_pos + 1.0) * (row_pos + 1.0) / (span * span))
    return fall_up, fall_down


def terms_of(anomaly, weights, pulls, factors):
    wide = anomaly.astype(F32)
    members, count = wide.shape
    lines = []
    for f in factors:
        lines.extend(thirds(to_line(pulls * f)))
    lines.append(jnp.zeros((16 - len(lines), count), BF16))
    vectors = against_rows(jnp.concatenate(lines, 0), anomaly)
    pad = jnp.zeros((7, members), F32)
    terms = []
    for i, f in enumerate(factors):
        matrix = against_rows((wide * to_line(weights * f)).astype(BF16), anomaly)
        side = vectors[3 * i : 3 * i + 1] + vectors[3 * i + 1 : 3 * i + 2]
        side = side + vectors[3 * i + 2 : 3 * i + 3]
        terms.append((matrix, jnp.concatenate([side, pad], 0)))
    return terms


def edge_kernel(states, obs, up, down):
    fall_up, fall_down = falls()
    members = states.shape[1]

    def put(out, factor):
        ((matrix, side),) = terms_of(*by_cell(states, obs), (factor,))
        out[:members] = matrix
        out[members:] = side

    @pl.when(pl.program_id(0) == 0)
    def _():
        put(up, fall_up)

    @pl.when(pl.program_id(0) == 1)
    def _():
        put(down, fall_down)


def curvature_kernel(states, obs, own):
    block = pl.program_id(0)
    blocks = pl.num_programs(0)
    members = states.shape[1]
    fall_up, fall_down = falls()
    terms = terms_of(*by_cell(states, obs), (jnp.ones_like(fall_up), fall_up, fall_down))

    @pl.when(block == 0)
    def _():
        own[...] = jnp.zeros_like(own)

    def add(place, term):
        own[place, :members] += term[0]
        own[place, members:] += term[1]

    add(block, terms[0])

    @pl.when(block > 0)
    def _():
        add(block - 1, terms[1])

    @pl.when(block < blocks - 1)
    def _():
        add(block + 1, terms[2])


def curvatures(states, obs):
    blocks, members, width = states.shape
    shape = (blocks, members + 8, members)
    return pl.pallas_call(
        curvature_kernel,
        grid=(blocks,),
        in_specs=[
            pl.BlockSpec((1, members, width), lambda i: (i, 0, 0)),
            pl.BlockSpec((1, 8, width), lambda i: (i, 0, 0)),
        ],
        out_specs=pl.BlockSpec(shape, lambda i: (0, 0, 0)),
        out_shape=jax.ShapeDtypeStruct(shape, F32),
        name="curvature",
        compiler_params=pltpu.CompilerParams(vmem_limit_bytes=16 << 20),
    )(states, obs)


def edge_curvatures(states, obs):
    blocks, members, width = states.shape
    shape = (members + 8, members)
    return pl.pallas_call(
        edge_kernel,
        grid=(2,),
        in_specs=[
            pl.BlockSpec((1, members, width), lambda i: (i * (blocks - 1), 0, 0)),
            pl.BlockSpec((1, 8, width), lambda i: (i * (blocks - 1), 0, 0)),
        ],
        out_specs=[pl.BlockSpec(shape, lambda i: (0, 0))] * 2,
        out_shape=[jax.ShapeDtypeStruct(shape, F32)] * 2,
        name="edge_curvature",
        compiler_params=pltpu.CompilerParams(vmem_limit_bytes=12 << 20),
    )(states, obs)


def transform_kernel(own, from_above, from_below, out, iterate, inverse):
    blocks, size, _ = iterate.shape
    row = lax.broadcasted_iota(jnp.int32, (size, size), 0)
    col = lax.broadcasted_iota(jnp.int32, (size, size), 1)
    diagonal = row == col

    def middle_of(x):
        return jnp.where(diagonal, 1.5 - 0.5 * x, -0.5 * x)

    norms, sides = [], []
    for b in range(blocks):
        matrix, side = own[b, :size], own[b, size:]
        if b == 0:
            matrix, side = matrix + from_above[:size], side + from_above[size:]
        if b == blocks - 1:
            matrix, side = matrix + from_below[:size], side + from_below[size:]
        matrix = matrix + jnp.where(diagonal, size - 1.0, 0.0)
        squares = jnp.sum(jnp.sum(matrix * matrix, axis=0, keepdims=True), axis=1, keepdims=True)
        norm = jnp.sqrt(squares)
        start = matrix / norm
        middle = middle_of(start)
        inverse[b] = middle
        iterate[b] = product(start, middle)
        norms.append(norm)
        sides.append(side)

    def sweep(i, carry):
        middles = [middle_of(product(inverse[b], iterate[b])) for b in range(blocks)]
        for b in range(blocks):
            both = product(jnp.concatenate([iterate[b], inverse[b]], 0), middles[b])
            iterate[b] = both[:size]
            inverse[b] = both[size:]
        return carry

    lax.fori_loop(0, ITERS - 2, sweep, 0)
    middles = [middle_of(product(inverse[b], iterate[b])) for b in range(blocks)]
    finals = [product(inverse[b], middles[b]) for b in range(blocks)]
    for b in range(blocks):
        flipped = finals[b].T
        inner = product(sides[b], flipped)
        shift = product(inner, flipped) / norms[b]
        out[b, :size] = flipped * (math.sqrt(size - 1.0) / jnp.sqrt(norms[b]))
        out[b, size:] = shift


def transforms(own, from_above, from_below):
    blocks, _, size = own.shape
    return pl.pallas_call(
        transform_kernel,
        out_shape=jax.ShapeDtypeStruct(own.shape, F32),
        scratch_shapes=[
            pltpu.VMEM((blocks, size, size), F32),
            pltpu.VMEM((blocks, size, size), F32),
        ],
        name="transform",
        compiler_params=pltpu.CompilerParams(vmem_limit_bytes=20 << 20),
    )(own, from_above, from_below)


def apply_kernel(share, states, weights, out):
    members = states.shape[1]
    cells = states[0]
    centre = jnp.sum(cells, axis=0, keepdims=True) * (1.0 / members)
    moved = product(weights[0], cells - centre)
    common = centre + moved[members : members + 1]
    kept = common.astype(BF16)
    moved = moved[:members] + (common - kept.astype(F32))
    for part in range(members // share):
        for r in range(ROWS):
            out[0, part, r * share : (r + 1) * share] = moved[
                part * share : (part + 1) * share, r * LANES : (r + 1) * LANES
            ].astype(BF16)
        out[0, part, ROWS * share :] = to_tile(kept)


def apply_transform(share, states, weights):
    blocks, members, width = states.shape
    lines = ROWS * (share + 1)
    return pl.pallas_call(
        partial(apply_kernel, share),
        grid=(blocks,),
        in_specs=[
            pl.BlockSpec((1, members, width), lambda i: (i, 0, 0)),
            pl.BlockSpec((1, members + 8, members), lambda i: (i, 0, 0)),
        ],
        out_specs=pl.BlockSpec((1, members // share, lines, LANES), lambda i: (i, 0, 0, 0)),
        out_shape=jax.ShapeDtypeStruct((blocks, members // share, lines, LANES), BF16),
        name="apply",
        compiler_params=pltpu.CompilerParams(vmem_limit_bytes=20 << 20),
    )(states, weights)


def unpack_kernel(share, chunk, out, stage):
    for part in range(PLANE):
        common = chunk[part, 0, ROWS * share :].astype(F32)
        for r in range(ROWS):
            field = chunk[part, 0, r * share : (r + 1) * share].astype(F32) + common[r : r + 1]
            for k in range(share // 8):
                stage[part, pl.ds(8 * ROWS * k + r, 8, stride=ROWS)] = field[8 * k : 8 * k + 8]
        out[:, part * LANES : (part + 1) * LANES] = stage[part]


def unpack(share, chunk):
    _, groups, lines, _ = chunk.shape
    return pl.pallas_call(
        partial(unpack_kernel, share),
        grid=(groups,),
        in_specs=[pl.BlockSpec((PLANE, 1, lines, LANES), lambda i: (0, i, 0, 0))],
        out_specs=pl.BlockSpec((share * ROWS, PLANE * LANES), lambda i: (0, i)),
        out_shape=jax.ShapeDtypeStruct((share * ROWS, groups * PLANE * LANES), F32),
        scratch_shapes=[pltpu.VMEM((PLANE, share * ROWS, LANES), F32)],
        name="unpack",
        compiler_params=pltpu.CompilerParams(vmem_limit_bytes=12 << 20),
    )(chunk)


def local(prior, drive, value, index, weight):
    members, rows, cols = prior.shape
    groups = lax.axis_size("member")
    planes = lax.axis_size("y")
    plane = lax.axis_index("y")
    upward = [(i + 1, i) for i in range(planes - 1)]
    downward = [(i, i + 1) for i in range(planes - 1)]
    me = jnp.stack([lax.axis_index("member"), lax.axis_index("zc")]).astype(jnp.int32)
    inside = jnp.stack([plane > 0, plane < planes - 1]).astype(F32)
    axes = ("zc", "member")
    tied = lax.optimization_barrier
    chunk, drive = tied((pack(prior), drive))
    outward = [
        (PLANE * i + edge, PLANE * j + edge)
        for edge, pairs in ((0, upward), (PLANE - 1, downward))
        for i, j in pairs
    ]
    extra = pack_extra(me, cols, drive, value, index, weight)
    outer_rows = lax.ppermute(extra, ("y", "zc"), outward)
    pieces = [jnp.concatenate([extra[d], outer_rows[d]], 0) for d in range(PLANE)]
    for d in range(1, PLANE):
        pieces[d] = lax.ppermute(
            pieces[d], "zc", [(i, (i + d) % PLANE) for i in range(PLANE)]
        )
    extra, force = forcing(me, pieces)
    chunk = lax.all_to_all(chunk, axes, 0, 0, tiled=True)
    cells = chunk.reshape(PLANE, groups, ROWS + 1, members, LANES)
    bottom = lax.ppermute(cells[0], "y", upward)
    top = lax.ppermute(cells[PLANE - 1], "y", downward)
    fields = forecast_inner(cells, force)
    states = forecast_outer(inside, top, bottom, force, *fields)
    up, down = edge_curvatures(states, extra)
    from_below = lax.ppermute(up, "y", upward)
    from_above = lax.ppermute(down, "y", downward)
    weights = transforms(curvatures(states, extra), from_above, from_below)
    analysed = apply_transform(members, states, weights)
    sent = analysed.reshape(PLANE * groups, *analysed.shape[2:])
    back = lax.all_to_all(sent, axes, 0, 0, tiled=True).reshape(analysed.shape)
    return unpack(members, back).reshape(members, rows, cols)


def solution(mesh):
    groups, spaces = mesh.devices.shape
    fine = Mesh(mesh.devices.reshape(groups, spaces // PLANE, PLANE), ("member", "y", "zc"))
    rows = ("y", "zc")
    return jax.shard_map(
        local,
        mesh=fine,
        in_specs=(
            P("member", rows, None),
            P(rows, None),
            P(rows, "member", None),
            P(rows, "member", None),
            P(rows, "member", None),
        ),
        out_specs=P("member", rows, None),
        check_vma=False,
    )
```
